128 devices in a mesh: span: 16 (over y, x_hi, core), tok: 8 (over x_lo, z).
Axes of the slice: x: 4 (x_hi: 2, x_lo: 2; x = x_hi * 2 + x_lo), y: 4, z: 4, core: 2. Of those that a mesh axis runs over, the one named last changes fastest.
Arguments:
- queries: bfloat16 [16, 512, 3072], P('span', 'tok'), may hold values from -9 to 9
- keys: bfloat16 [16, 512, 3072], P('span', 'tok'), may hold values from -9 to 9
- values: bfloat16 [16, 512, 3072], P('span', 'tok'), may hold values from -6 to 6
- levels: int32 [16], P('span'), may hold values from 0 to 15
- retiring: int32 [1], replicated, may hold values from 0 to 15
- block_mask: int32 [16, 16], P('span'), may hold values 0 or 1
- gates: float32 [16, 3072], replicated, may hold values from 0.5 to 2
Outputs:
- attended: bfloat16 [16, 512, 3072], P('span', 'tok')
The draws below stay inside these ranges and needn't reach their ends.
All inputs are finite; a program needn't handle non-finite values. No bound on the sum of `block_mask` on one device may be relied on, other than what follows from the above.
Results may differ from the reference program's by a relative error of at most 0.0085.
Values may be sent and summed in bfloat16 or wider, within the bound.
No kernel may reach another device: no remote copies, remote signals or barrier semaphores. Data moves between devices by JAX's collectives and lax.ppermute only.
A program may use at most 128 MiB of HBM per device.

```python
import math
import jax
import jax.numpy as jnp
from jax import lax

HEADS = 24
HEAD_DIM = 128
LEVELS = 16
FEAT = 3072
SPANS = 16
CTOK = 512


def base_draw(key, salt):
    base = jax.random.truncated_normal(jax.random.fold_in(key, salt), -4.0, 4.0, (SPANS, CTOK, HEADS * HEAD_DIM), jnp.float32)
    return base


def draw_queries(key, part):
    base = base_draw(key, 1)
    return base.astype(jnp.bfloat16)


def draw_keys(key, part):
    base = base_draw(key, 2)
    return base.astype(jnp.bfloat16)


def place_ends(values, rng, low, high):
    index_at = [jax.random.randint(jax.random.fold_in(rng, axis), (), 0, length) for axis, length in enumerate(values.shape)]
    widest = values.shape.index(max(values.shape))
    beside = index_at[:widest] + [(index_at[widest] + 1) % values.shape[widest]] + index_at[widest + 1:]
    return values.at[tuple(index_at)].set(low).at[tuple(beside)].set(high)


def block_scale(stream_key, shape, cuts, low, high):
    factor_of = 1.0
    for axis_at, blocks in cuts:
        draws = jax.random.uniform(jax.random.fold_in(jax.random.fold_in(stream_key, 6), axis_at), (blocks,), jnp.float32, low / len(cuts), high / len(cuts))
        factor_of = factor_of * jnp.repeat(jnp.exp(draws), shape[axis_at] // blocks).reshape((-1,) + (1,) * (len(shape) - 1 - axis_at))
    return factor_of


def centred(stream_key, dims, scale, bound, shards=(), kind=jnp.bfloat16):
    entries = scale * jax.random.normal(stream_key, dims, jnp.float32)
    if shards:
        entries = entries * block_scale(stream_key, dims, shards, -0.22, 0.18)
    return jnp.clip(entries, -bound, bound).astype(kind)


def setup_inputs(seed: int = 0) -> dict:
    seeds = jax.random.split(jax.random.key(seed), 8)
    queries = draw_queries(jax.random.fold_in(seeds[7], 71), 0)
    keys = draw_keys(jax.random.fold_in(seeds[7], 71), 0)
    values = centred(seeds[2], (SPANS, CTOK, FEAT), 1.0, 6.0, ((0, 16), (1, 8)))
    levels = place_ends(jax.random.randint(seeds[3], (SPANS,), 0, LEVELS), jax.random.fold_in(seeds[3], 1), 0, LEVELS - 1).astype(jnp.int32)
    retiring = jax.random.randint(seeds[4], (1,), 0, SPANS).astype(jnp.int32)
    block_mask = place_ends((jax.random.randint(seeds[5], (SPANS, SPANS), 0, 4) < 3).astype(jnp.int32), jax.random.fold_in(seeds[5], 1), 0, 1)
    gates = jnp.clip(jnp.exp(jax.random.uniform(seeds[6], (LEVELS, FEAT), jnp.float32, math.log(0.5), math.log(2.0))), 0.5, 2.0)
    return {"queries": queries, "keys": keys, "values": values, "levels": levels, "retiring": retiring, "block_mask": block_mask, "gates": gates}


def reference(queries, keys, values, levels, retiring, block_mask, gates):
    spans = queries.shape[0]
    ctok = queries.shape[1]
    slots = jnp.arange(spans, dtype=jnp.int32)
    order = (slots - retiring[0]) % spans
    allowed = (slots[:, None] == slots[None, :]) | ((block_mask == 1) & (order[None, :] < order[:, None]))
    all_keys = keys.reshape(spans * ctok, HEADS, HEAD_DIM)
    all_values = values.reshape(spans * ctok, HEADS, HEAD_DIM)
    scale = jnp.float32(HEAD_DIM ** -0.5)

    def per_span(slot):
        query = queries[slot].reshape(ctok, HEADS, HEAD_DIM)
        keep = jnp.repeat(allowed[slot], ctok)

        def per_head(head):
            score = jnp.dot(query[:, head], all_keys[:, head].T, preferred_element_type=jnp.float32) * scale
            score = jnp.where(keep[None, :], score, -jnp.inf)
            weight = jnp.exp(score - jnp.max(score, axis=-1, keepdims=True))
            total = jnp.sum(weight, axis=-1)
            mixed = jnp.dot(weight.astype(jnp.bfloat16), all_values[:, head], preferred_element_type=jnp.float32)
            return mixed / total[:, None]

        mixed = lax.map(per_head, jnp.arange(HEADS, dtype=jnp.int32))
        mixed = jnp.transpose(mixed, (1, 0, 2)).reshape(ctok, HEADS * HEAD_DIM)
        return (mixed * gates[levels[slot]][None, :]).astype(jnp.bfloat16)

    return lax.map(per_span, slots)
```

```python
import functools

import jax
import jax.numpy as jnp
from jax import lax
from jax.experimental import pallas as pl
from jax.experimental.pallas import tpu as pltpu
from jax.sharding import PartitionSpec as P

HEAD_DIM = 128
SPANS = 16
ROWS = 64
GROUP = 8
HEADS_DEV = 3
WIDTH = HEADS_DEV * HEAD_DIM
RING = 4
SET = GROUP * ROWS
META = 32
PARTS = ((0, 1, 2),)
STEP = 4
LOG2E = 1.4426950408889634


BOTH = ("span", "tok")
VMEM = pl.BlockSpec(memory_space=pltpu.VMEM)
SMEM = pl.BlockSpec(memory_space=pltpu.SMEM)


def device_at(x, y, z, core):
    return (y * 4 + (x // 2) * 2 + core) * 8 + (x % 2) * 4 + z


def moved(array, dx=0, dy=0, dz=0, core=0, flip=0):
    pairs = []
    for x in range(4):
        for y in range(4):
            for z in range(4):
                for c in range(2):
                    there = device_at((x + dx) % 4 ^ flip, (y + dy) % 4, (z + dz) % 4, c ^ core)
                    pairs.append((device_at(x, y, z, c), there))
    return lax.ppermute(array, BOTH, pairs)


def call(kernel, shapes, specs, scratch=()):
    return pl.pallas_call(
        kernel,
        out_shape=shapes,
        in_specs=specs,
        out_specs=jax.tree.map(lambda unused: VMEM, shapes),
        scratch_shapes=scratch,
    )


def shape(rows, columns, dtype=jnp.bfloat16):
    return jax.ShapeDtypeStruct((rows, columns), dtype)


def pack_kernel(at_ref, q_ref, k_ref, v_ref, meta_ref, *out_refs):
    for j in range(GROUP):
        columns = pl.ds(pl.multiple_of(at_ref[j] * WIDTH, HEAD_DIM), WIDTH)
        for i, ref in enumerate((q_ref, k_ref, v_ref)):
            out_refs[j][i * ROWS : (i + 1) * ROWS, :] = ref[:, columns]
        out_refs[j][3 * ROWS :, :] = meta_ref[...]


def spread_kernel(*refs):
    in_refs, out_refs = refs[:GROUP], refs[GROUP:]
    for j in range(GROUP):
        ref = in_refs[j]
        for p, part in enumerate(PARTS):
            q_ref, kv_ref = out_refs[2 * p], out_refs[2 * p + 1]
            for i, h in enumerate(part):
                columns = slice(h * HEAD_DIM, (h + 1) * HEAD_DIM)
                q_ref[i * SET + j * ROWS : i * SET + (j + 1) * ROWS, :] = ref[0:ROWS, columns]
                for t in range(2):
                    base = (2 * i + t) * SET + j * ROWS
                    kv_ref[base : base + ROWS, :] = ref[(t + 1) * ROWS : (t + 2) * ROWS, columns]
        row = ref[3 * ROWS : 3 * ROWS + 16, 0:HEAD_DIM].astype(jnp.float32)
        out_refs[-1][j : j + 1, :] = row[0:1]


def attend_kernel(count, table_ref, *refs):
    q_refs, kv_refs = refs[:RING], refs[RING : 2 * RING]
    out_refs = refs[2 * RING : 3 * RING]
    k_all, v_all, lse_ref = refs[3 * RING :]
    factor = jnp.float32(HEAD_DIM ** (-0.5) * LOG2E)
    rows = RING * ROWS
    wide = 2 * ROWS
    lanes = lax.broadcasted_iota(jnp.int32, (ROWS, HEAD_DIM), 1)
    eye = lanes == lax.broadcasted_iota(jnp.int32, (ROWS, HEAD_DIM), 0)

    def head(h, unused):
        base = pl.multiple_of(h * 2 * SET, SET)
        for core in range(2):
            for j in range(GROUP):
                for half in range(2):
                    source = kv_refs[2 * core + half]
                    to = (core * GROUP + j) * wide + half * ROWS
                    k_all[to : to + ROWS, :] = source[pl.ds(base + j * ROWS, ROWS), :]
                    v_all[to : to + ROWS, :] = source[pl.ds(base + SET + j * ROWS, ROWS), :]

        def span(j, unused):
            start = pl.multiple_of(h * SET + j * ROWS, ROWS)
            query = jnp.concatenate([ref[pl.ds(start, ROWS), :] for ref in q_refs], axis=0)
            seen = table_ref[SPANS * GROUP + j]

            def step(g, carry):
                top, total, acc = carry
                pieces_k, pieces_v, keep = [], [], []
                for u in range(STEP):
                    at = pl.multiple_of(table_ref[j * SPANS + g * STEP + u] * wide, wide)
                    pieces_k.append(k_all[pl.ds(at, wide), :])
                    pieces_v.append(v_all[pl.ds(at, wide), :])
                    keep.append(g * STEP + u < seen)
                score = lax.dot_general(
                    query,
                    jnp.concatenate(pieces_k, axis=0),
                    (((1,), (1,)), ((), ())),
                    preferred_element_type=jnp.float32,
                )
                blocks = []
                for u in range(STEP):
                    block = score[:, u * wide : (u + 1) * wide]
                    blocks.append(block if u == 0 else jnp.where(keep[u], block, -1e30))
                largest = functools.reduce(jnp.maximum, blocks)
                new_top = jnp.maximum(top, jnp.max(largest, axis=1, keepdims=True))
                shrink = jnp.exp2((top - new_top) * factor)
                weights = [jnp.exp2((block - new_top) * factor) for block in blocks]
                total = total * shrink + functools.reduce(jnp.add, weights)
                weight = jnp.concatenate([w.astype(jnp.bfloat16) for w in weights], axis=1)
                acc = acc * shrink + jnp.dot(
                    weight, jnp.concatenate(pieces_v, axis=0), preferred_element_type=jnp.float32
                )
                return new_top, total, acc

            top, total, acc = lax.fori_loop(
                0,
                (seen + STEP - 1) // STEP,
                step,
                (
                    jnp.full((rows, 1), -1e30, jnp.float32),
                    jnp.zeros((rows, HEAD_DIM), jnp.float32),
                    jnp.zeros((rows, HEAD_DIM), jnp.float32),
                ),
            )
            total = jnp.sum(total, axis=1, keepdims=True)
            mixed = (acc / total).astype(jnp.bfloat16)
            lse = top * factor + jnp.log2(total)
            place = pl.multiple_of(h * (SET + META) + j * ROWS, 32)
            for d in range(RING):
                out_refs[d][pl.ds(place, ROWS), :] = mixed[d * ROWS : (d + 1) * ROWS]
                column = jnp.where(eye, lse[d * ROWS : (d + 1) * ROWS], 0.0)
                lse_ref[d, pl.ds(j, 1), :] = jnp.sum(column, axis=0, keepdims=True)
            return unused

        lax.fori_loop(0, GROUP, span, 0)
        place = pl.multiple_of(h * (SET + META) + SET, 32)
        for d in range(RING):
            value = lse_ref[d]
            high = value.astype(jnp.bfloat16).astype(jnp.float32)
            middle = (value - high).astype(jnp.bfloat16).astype(jnp.float32)
            low = value - high - middle
            out_refs[d][pl.ds(place, META), :] = jnp.concatenate(
                [high, middle, low, jnp.zeros_like(low)], axis=0
            ).astype(jnp.bfloat16)
        return unused

    lax.fori_loop(0, count, head, 0)


def combine_kernel(*refs):
    out_refs = refs[-GROUP:]
    lanes = lax.broadcasted_iota(jnp.int32, (ROWS, HEAD_DIM), 1)
    eye = lanes == lax.broadcasted_iota(jnp.int32, (ROWS, HEAD_DIM), 0)
    for p, part in enumerate(PARTS):
        pieces = refs[p * RING : (p + 1) * RING]
        for i, h in enumerate(part):
            base = i * (SET + META)
            lse = []
            for ref in pieces:
                coded = ref[base + SET : base + SET + META, :].astype(jnp.float32)
                lse.append(coded[0:8] + coded[8:16] + coded[16:24])
            top = functools.reduce(jnp.maximum, lse)
            shares = [jnp.exp2(value - top) for value in lse]
            total = functools.reduce(jnp.add, shares)
            shares = [value / total for value in shares]
            for j in range(GROUP):
                mixed = jnp.zeros((ROWS, HEAD_DIM), jnp.float32)
                for ref, share in zip(pieces, shares):
                    column = jnp.sum(jnp.where(eye, share[j : j + 1], 0.0), axis=1, keepdims=True)
                    rows = ref[base + j * ROWS : base + (j + 1) * ROWS, :]
                    mixed = mixed + column * rows.astype(jnp.float32)
                out_refs[j][:, h * HEAD_DIM : (h + 1) * HEAD_DIM] = mixed.astype(jnp.bfloat16)


def finish_kernel(at_ref, level_ref, gates_ref, *refs):
    out_ref = refs[-1]
    for j in range(GROUP):
        columns = pl.ds(pl.multiple_of(at_ref[j] * WIDTH, HEAD_DIM), WIDTH)
        gate = gates_ref[pl.ds(level_ref[0], 1), columns]
        out_ref[:, columns] = (refs[j][...].astype(jnp.float32) * gate).astype(jnp.bfloat16)


def see_table(slots, retiring, mask):
    order = (slots - retiring[0]) % SPANS
    names = jnp.arange(SPANS, dtype=jnp.int32)
    picked = (slots[:, None] == names[None, :]).astype(jnp.float32)
    masked = jnp.sum(mask[:, None, :SPANS] * picked[None], axis=-1) > 0.5
    older = order[None, :] < order[:GROUP, None]
    same = slots[None, :] == slots[:GROUP, None]
    sees = same | masked & older
    before = names[None, :] < names[:, None]
    rank = jnp.sum((sees[:, None, :] & before[None]).astype(jnp.int32), axis=-1)
    chosen = sees[:, None, :] & (rank[:, None, :] == names[None, :, None])
    listed = jnp.sum(jnp.where(chosen, names[None, None, :], 0), axis=-1)
    counts = jnp.sum(sees.astype(jnp.int32), axis=-1)
    return jnp.concatenate([listed.reshape(-1), counts])


def local(queries, keys, values, levels, retiring, block_mask, gates):
    span = lax.axis_index("span").astype(jnp.int32)
    y, half, core = span // 4, span // 2 % 2, span % 2
    hop = jnp.arange(GROUP, dtype=jnp.int32)
    hop_y, hop_half = hop // 2, hop % 2
    target = (y + hop_y) % 4 * 2 + (half ^ hop_half)
    source = (y - hop_y) % 4 * 4 + (half ^ hop_half) * 2
    slots = jnp.concatenate([source + core, source + 1 - core])
    hops = [dict(dy=j // 2, dx=2 * (j % 2)) for j in range(GROUP)]
    backs = [dict(dy=-(j // 2), dx=2 * (j % 2)) for j in range(GROUP)]

    meta = jnp.pad(block_mask.astype(jnp.bfloat16), ((0, 15), (0, WIDTH - SPANS)))
    packed = call(
        pack_kernel,
        [shape(3 * ROWS + 16, WIDTH)] * GROUP,
        [SMEM, VMEM, VMEM, VMEM, VMEM],
    )(target, queries[0], keys[0], values[0], meta)
    shared = [packed[0]] + [moved(packed[j], **hops[j]) for j in range(1, GROUP)]

    shapes = []
    for part in PARTS:
        shapes += [shape(len(part) * SET, HEAD_DIM), shape(len(part) * 2 * SET, HEAD_DIM)]
    spread = call(
        spread_kernel, shapes + [shape(GROUP, HEAD_DIM, jnp.float32)], [VMEM] * GROUP
    )(*shared)
    table = see_table(slots, retiring, spread[-1])

    pieces = []
    for p, part in enumerate(PARTS):
        own_q, own_kv = spread[2 * p], spread[2 * p + 1]
        far_kv = moved(own_kv, flip=1)
        kv = [own_kv, far_kv, moved(own_kv, core=1), moved(far_kv, core=1)]
        q = [own_q] + [moved(own_q, dz=d) for d in range(1, RING)]
        count = len(part)
        parts = call(
            functools.partial(attend_kernel, count),
            [shape(count * (SET + META), HEAD_DIM)] * RING,
            [SMEM] + [VMEM] * (2 * RING),
            [
                pltpu.VMEM((2 * SPANS * ROWS, HEAD_DIM), jnp.bfloat16),
                pltpu.VMEM((2 * SPANS * ROWS, HEAD_DIM), jnp.bfloat16),
                pltpu.VMEM((RING, GROUP, HEAD_DIM), jnp.float32),
            ],
        )(table, *q, *kv)
        pieces += [parts[0]] + [moved(parts[d], dz=-d) for d in range(1, RING)]

    mixed = call(combine_kernel, [shape(ROWS, WIDTH)] * GROUP, [VMEM] * len(pieces))(*pieces)
    returned = [mixed[0]] + [moved(mixed[j], **backs[j]) for j in range(1, GROUP)]
    result = call(finish_kernel, shape(ROWS, GROUP * WIDTH), [SMEM, SMEM] + [VMEM] * (GROUP + 1))(
        target, levels, gates, *returned
    )
    return result[None]


def solution(mesh):
    return jax.shard_map(
        local,
        mesh=mesh,
        in_specs=(
            P("span", "tok", None),
            P("span", "tok", None),
            P("span", "tok", None),
            P("span"),
            P(),
            P("span", None),
            P(),
        ),
        out_specs=P("span", "tok", None),
        check_vma=False,
    )
```

```python
import functools

import jax
import jax.numpy as jnp
from jax import lax
from jax.experimental import pallas as pl
from jax.experimental.pallas import tpu as pltpu
from jax.sharding import PartitionSpec as P

HEAD_DIM = 128
SPANS = 16
ROWS = 64
GROUP = 8
HEADS_DEV = 3
WIDTH = HEADS_DEV * HEAD_DIM
RING = 4
SET = GROUP * ROWS
META = 32
PARTS = ((0, 1, 2),)
TILE = 2 * ROWS
TILES = 16
STEP = 4
TOGETHER = 1
LOG2E = 1.4426950408889634


BOTH = ("span", "tok")
VMEM = pl.BlockSpec(memory_space=pltpu.VMEM)
SMEM = pl.BlockSpec(memory_space=pltpu.SMEM)


def device_at(x, y, z, core):
    return (y * 4 + (x // 2) * 2 + core) * 8 + (x % 2) * 4 + z


def moved(array, dx=0, dy=0, dz=0, core=0, swap=0):
    pairs = []
    for x in range(4):
        for y in range(4):
            for z in range(4):
                for c in range(2):
                    mx, mz = (dz, dx) if swap and c else (dx, dz)
                    there = device_at((x + mx) % 4, (y + dy) % 4, (z + mz) % 4, c ^ core)
                    pairs.append((device_at(x, y, z, c), there))
    return lax.ppermute(array, BOTH, pairs)


def call(kernel, shapes, specs, scratch=()):
    return pl.pallas_call(
        kernel,
        out_shape=shapes,
        in_specs=specs,
        out_specs=jax.tree.map(lambda unused: VMEM, shapes),
        scratch_shapes=scratch,
    )


def shape(rows, columns, dtype=jnp.bfloat16):
    return jax.ShapeDtypeStruct((rows, columns), dtype)


def pack_kernel(at_ref, q_ref, k_ref, v_ref, meta_ref, *out_refs):
    for j in range(GROUP):
        columns = pl.ds(pl.multiple_of(at_ref[j] * WIDTH, HEAD_DIM), WIDTH)
        for i, ref in enumerate((q_ref, k_ref, v_ref)):
            out_refs[j][i * ROWS : (i + 1) * ROWS, :] = ref[:, columns]
        out_refs[j][3 * ROWS :, :] = meta_ref[...]


def spread_kernel(*refs):
    in_refs, out_refs = refs[:GROUP], refs[GROUP:]
    for j in range(GROUP):
        ref = in_refs[j]
        for p, part in enumerate(PARTS):
            q_ref, kv_ref = out_refs[2 * p], out_refs[2 * p + 1]
            for i, h in enumerate(part):
                columns = slice(h * HEAD_DIM, (h + 1) * HEAD_DIM)
                q_ref[i * SET + j * ROWS : i * SET + (j + 1) * ROWS, :] = ref[0:ROWS, columns]
                for t in range(2):
                    base = (2 * i + t) * SET + j * ROWS
                    kv_ref[base : base + ROWS, :] = ref[(t + 1) * ROWS : (t + 2) * ROWS, columns]
        row = ref[3 * ROWS : 3 * ROWS + 16, 0:HEAD_DIM].astype(jnp.float32)
        out_refs[-1][j : j + 1, :] = row[0:1]


def attend_kernel(count, table_ref, *refs):
    q_refs, kv_refs = refs[:RING], refs[RING : 2 * RING]
    out_refs = refs[2 * RING : 3 * RING]
    q_all, k_all, v_all, o_all, lse_ref = refs[3 * RING :]
    factor = jnp.float32(HEAD_DIM ** (-0.5) * LOG2E)
    eye = lax.broadcasted_iota(jnp.int32, (TILE, TILE), 1) == lax.broadcasted_iota(
        jnp.int32, (TILE, TILE), 0
    )
    limits = TILES * TILES
    q_place = [table_ref[limits + TILES + d] for d in range(RING)]
    k_place = [table_ref[limits + TILES + RING + d] for d in range(RING)]
    for h in range(count):
        for d in range(RING):
            for j in range(GROUP):
                rows = slice(h * SET + j * ROWS, h * SET + (j + 1) * ROWS)
                to = pl.multiple_of(j * RING * ROWS + q_place[d] * ROWS, ROWS)
                q_all[h, pl.ds(to, ROWS), :] = q_refs[d][rows, :]
                to = pl.multiple_of(j * RING * ROWS + k_place[d] * ROWS, ROWS)
                base = 2 * h * SET + j * ROWS
                k_all[h, pl.ds(to, ROWS), :] = kv_refs[d][base : base + ROWS, :]
                v_all[h, pl.ds(to, ROWS), :] = kv_refs[d][base + SET : base + SET + ROWS, :]

    def tiles(first, unused):
        picks = [first * TOGETHER + t for t in range(TOGETHER)]
        seen = [table_ref[limits + i] for i in picks]
        trips = functools.reduce(jnp.maximum, seen)
        chains = [(t, h) for t in range(TOGETHER) for h in range(count)]
        starts = [pl.multiple_of(i * TILE, TILE) for i in picks]

        def step(g, carry):
            places = [
                [
                    pl.multiple_of(table_ref[i * TILES + g * STEP + u] * TILE, TILE)
                    for u in range(STEP)
                ]
                for i in picks
            ]
            scores = []
            for t, h in chains:
                scores.append(
                    lax.dot_general(
                        q_all[h, pl.ds(starts[t], TILE), :],
                        jnp.concatenate([k_all[h, pl.ds(at, TILE), :] for at in places[t]], axis=0),
                        (((1,), (1,)), ((), ())),
                        preferred_element_type=jnp.float32,
                    )
                )
            result = []
            for (t, h), score, (top, total, acc) in zip(chains, scores, carry):
                blocks = [
                    jnp.where(
                        g * STEP + u < seen[t], score[:, u * TILE : (u + 1) * TILE], -1e30
                    )
                    for u in range(STEP)
                ]
                largest = functools.reduce(jnp.maximum, blocks)
                new_top = jnp.maximum(top, jnp.max(largest, axis=1, keepdims=True))
                shrink = jnp.exp2((top - new_top) * factor)
                weights = [jnp.exp2((block - new_top) * factor) for block in blocks]
                total = total * shrink + functools.reduce(jnp.add, weights)
                weight = jnp.concatenate([w.astype(jnp.bfloat16) for w in weights], axis=1)
                acc = acc * shrink + jnp.dot(
                    weight,
                    jnp.concatenate([v_all[h, pl.ds(at, TILE), :] for at in places[t]], axis=0),
                    preferred_element_type=jnp.float32,
                )
                result.append((new_top, total, acc))
            return result

        empty = (
            jnp.full((TILE, 1), -1e30, jnp.float32),
            jnp.zeros((TILE, HEAD_DIM), jnp.float32),
            jnp.zeros((TILE, HEAD_DIM), jnp.float32),
        )
        final = lax.fori_loop(0, (trips + STEP - 1) // STEP, step, [empty] * len(chains))
        for (t, h), (top, total, acc) in zip(chains, final):
            total = jnp.sum(total, axis=1, keepdims=True)
            total = jnp.where(total > 0.0, total, 1.0)
            o_all[h, pl.ds(starts[t], TILE), :] = (acc / total).astype(jnp.bfloat16)
            column = jnp.where(eye, top * factor + jnp.log2(total), 0.0)
            row = jnp.sum(column, axis=0, keepdims=True)
            lse_ref[h, picks[t] % 2, pl.ds(picks[t] // 2, 1), :] = row
        return unused

    lax.fori_loop(0, TILES // TOGETHER, tiles, 0)
    for h in range(count):
        for d in range(RING):
            base = h * (SET + META)
            for j in range(GROUP):
                at = pl.multiple_of(j * RING * ROWS + q_place[d] * ROWS, ROWS)
                out_refs[d][base + j * ROWS : base + (j + 1) * ROWS, :] = o_all[
                    h, pl.ds(at, ROWS), :
                ]
            value = lse_ref[h, q_place[d] // 2]
            high = value.astype(jnp.bfloat16).astype(jnp.float32)
            middle = (value - high).astype(jnp.bfloat16).astype(jnp.float32)
            low = value - high - middle
            out_refs[d][base + SET : base + SET + META, :] = jnp.concatenate(
                [high, middle, low, jnp.zeros_like(low)], axis=0
            ).astype(jnp.bfloat16)


def combine_kernel(table_ref, *refs):
    out_refs = refs[-GROUP:]
    shift = table_ref[TILES * TILES + TILES] % 2 * ROWS
    lanes = lax.broadcasted_iota(jnp.int32, (ROWS, HEAD_DIM), 1)
    eye = lanes == lax.broadcasted_iota(jnp.int32, (ROWS, HEAD_DIM), 0) + shift
    for p, part in enumerate(PARTS):
        pieces = refs[p * RING : (p + 1) * RING]
        for i, h in enumerate(part):
            base = i * (SET + META)
            lse = []
            for ref in pieces:
                coded = ref[base + SET : base + SET + META, :].astype(jnp.float32)
                lse.append(coded[0:8] + coded[8:16] + coded[16:24])
            top = functools.reduce(jnp.maximum, lse)
            shares = [jnp.exp2(value - top) for value in lse]
            total = functools.reduce(jnp.add, shares)
            shares = [value / total for value in shares]
            for j in range(GROUP):
                mixed = jnp.zeros((ROWS, HEAD_DIM), jnp.float32)
                for ref, share in zip(pieces, shares):
                    column = jnp.sum(jnp.where(eye, share[j : j + 1], 0.0), axis=1, keepdims=True)
                    rows = ref[base + j * ROWS : base + (j + 1) * ROWS, :]
                    mixed = mixed + column * rows.astype(jnp.float32)
                out_refs[j][:, h * HEAD_DIM : (h + 1) * HEAD_DIM] = mixed.astype(jnp.bfloat16)


def finish_kernel(at_ref, level_ref, gates_ref, *refs):
    out_ref = refs[-1]
    for j in range(GROUP):
        columns = pl.ds(pl.multiple_of(at_ref[j] * WIDTH, HEAD_DIM), WIDTH)
        gate = gates_ref[pl.ds(level_ref[0], 1), columns]
        out_ref[:, columns] = (refs[j][...].astype(jnp.float32) * gate).astype(jnp.bfloat16)


def see_table(q_slots, k_slots, retiring, mask, places):
    names = jnp.arange(TILES, dtype=jnp.int32)
    q_order = (q_slots - retiring[0]) % SPANS
    k_order = (k_slots - retiring[0]) % SPANS
    slots = jnp.arange(SPANS, dtype=jnp.int32)
    picked = (k_slots[:, None] == slots[None, :]).astype(jnp.float32)
    masked = jnp.sum(mask[:, None, :SPANS] * picked[None], axis=-1) > 0.5
    older = k_order[None, :] < q_order[:, None]
    same = k_slots[None, :] == q_slots[:, None]
    sees = same | masked & older
    before = names[None, :] < names[:, None]
    rank = jnp.sum((sees[:, None, :] & before[None]).astype(jnp.int32), axis=-1)
    chosen = sees[:, None, :] & (rank[:, None, :] == names[None, :, None])
    listed = jnp.sum(jnp.where(chosen, names[None, None, :], 0), axis=-1)
    counts = jnp.sum(sees.astype(jnp.int32), axis=-1)
    return jnp.concatenate([listed.reshape(-1), counts, places])


def local(queries, keys, values, levels, retiring, block_mask, gates):
    span = lax.axis_index("span").astype(jnp.int32)
    token = lax.axis_index("tok").astype(jnp.int32)
    y, half, core = span // 4, span // 2 % 2, span % 2
    x, z = half * 2 + token // RING, token % RING
    hop = jnp.arange(GROUP, dtype=jnp.int32)
    target = (y + hop // 2) % 4 * 2 + (core ^ hop % 2)
    hops = [dict(dy=j // 2, core=j % 2) for j in range(GROUP)]
    backs = [dict(dy=-(j // 2), core=j % 2) for j in range(GROUP)]

    meta = jnp.pad(block_mask.astype(jnp.bfloat16), ((0, 15), (0, WIDTH - SPANS)))
    packed = call(
        pack_kernel,
        [shape(3 * ROWS + 16, WIDTH)] * GROUP,
        [SMEM, VMEM, VMEM, VMEM, VMEM],
    )(target, queries[0], keys[0], values[0], meta)
    shared = [packed[0]] + [moved(packed[j], **hops[j]) for j in range(1, GROUP)]

    shapes = []
    for part in PARTS:
        shapes += [shape(len(part) * SET, HEAD_DIM), shape(len(part) * 2 * SET, HEAD_DIM)]
    spread = call(
        spread_kernel, shapes + [shape(GROUP, HEAD_DIM, jnp.float32)], [VMEM] * GROUP
    )(*shared)

    tile = jnp.arange(TILES, dtype=jnp.int32)
    base = (y - tile // 4) % 4 * 4 + (core ^ tile // 2 % 2)
    wide_slots, near_slots = base + 2 * (tile % 2), base + 2 * half
    near_mask = jnp.repeat(spread[-1], 2, axis=0)
    far_mask = jnp.repeat(moved(spread[-1], dx=2), 2, axis=0)
    wide_mask = jnp.where((tile % 2 == half)[:, None], near_mask, far_mask)
    first = core == 0
    ring = jnp.arange(RING, dtype=jnp.int32)
    table = see_table(
        jnp.where(first, wide_slots, near_slots),
        jnp.where(first, near_slots, wide_slots),
        retiring,
        jnp.where(first, wide_mask, near_mask),
        jnp.concatenate(
            [(jnp.where(first, x, z) - ring) % RING, (jnp.where(first, z, x) - ring) % RING]
        ),
    )

    pieces = []
    for p, part in enumerate(PARTS):
        own_q, own_kv = spread[2 * p], spread[2 * p + 1]
        q = [own_q] + [moved(own_q, dx=d, swap=1) for d in range(1, RING)]
        kv = [own_kv] + [moved(own_kv, dz=d, swap=1) for d in range(1, RING)]
        count = len(part)
        all_rows = pltpu.VMEM((count, RING * SET, HEAD_DIM), jnp.bfloat16)
        parts = call(
            functools.partial(attend_kernel, count),
            [shape(count * (SET + META), HEAD_DIM)] * RING,
            [SMEM] + [VMEM] * (2 * RING),
            [all_rows] * 4 + [pltpu.VMEM((count, 2, GROUP, HEAD_DIM), jnp.float32)],
        )(table, *q, *kv)
        pieces += [parts[0]] + [moved(parts[d], dx=-d, swap=1) for d in range(1, RING)]

    mixed = call(
        combine_kernel, [shape(ROWS, WIDTH)] * GROUP, [SMEM] + [VMEM] * len(pieces)
    )(table, *pieces)
    returned = [mixed[0]] + [moved(mixed[j], **backs[j]) for j in range(1, GROUP)]
    result = call(finish_kernel, shape(ROWS, GROUP * WIDTH), [SMEM, SMEM] + [VMEM] * (GROUP + 1))(
        target, levels, gates, *returned
    )
    return result[None]


def solution(mesh):
    return jax.shard_map(
        local,
        mesh=mesh,
        in_specs=(
            P("span", "tok", None),
            P("span", "tok", None),
            P("span", "tok", None),
            P("span"),
            P(),
            P("span", None),
            P(),
        ),
        out_specs=P("span", "tok", None),
        check_vma=False,
    )
```

```python
import functools

import jax
import jax.numpy as jnp
from jax import lax
from jax.experimental import pallas as pl
from jax.experimental.pallas import tpu as pltpu
from jax.sharding import PartitionSpec as P

HEAD_DIM = 128
SPANS = 16
ROWS = 64
GROUP = 8
HEADS_DEV = 3
WIDTH = HEADS_DEV * HEAD_DIM
RING = 4
SET = GROUP * ROWS
META = 32
PARTS = ((0,), (1,), (2,))
TILE = 2 * ROWS
TILES = 16
STEP = 4
LOG2E = 1.4426950408889634


BOTH = ("span", "tok")
VMEM = pl.BlockSpec(memory_space=pltpu.VMEM)
SMEM = pl.BlockSpec(memory_space=pltpu.SMEM)


def device_at(x, y, z, core):
    return (y * 4 + (x // 2) * 2 + core) * 8 + (x % 2) * 4 + z


def moved(array, dx=0, dy=0, dz=0, core=0, swap=0):
    pairs = []
    for x in range(4):
        for y in range(4):
            for z in range(4):
                for c in range(2):
                    mx, mz = (dz, dx) if swap and c else (dx, dz)
                    there = device_at((x + mx) % 4, (y + dy) % 4, (z + mz) % 4, c ^ core)
                    pairs.append((device_at(x, y, z, c), there))
    return lax.ppermute(array, BOTH, pairs)


def call(kernel, shapes, specs, scratch=()):
    return pl.pallas_call(
        kernel,
        out_shape=shapes,
        in_specs=specs,
        out_specs=jax.tree.map(lambda unused: VMEM, shapes),
        scratch_shapes=scratch,
    )


def shape(rows, columns, dtype=jnp.bfloat16):
    return jax.ShapeDtypeStruct((rows, columns), dtype)


def pack_kernel(at_ref, q_ref, k_ref, v_ref, meta_ref, *out_refs):
    for j in range(GROUP):
        columns = pl.ds(pl.multiple_of(at_ref[j] * WIDTH, HEAD_DIM), WIDTH)
        for i, ref in enumerate((q_ref, k_ref, v_ref)):
            out_refs[j][i * ROWS : (i + 1) * ROWS, :] = ref[:, columns]
        out_refs[j][3 * ROWS :, :] = meta_ref[...]


def spread_kernel(*refs):
    in_refs, out_refs = refs[:GROUP], refs[GROUP:]
    for j in range(GROUP):
        ref = in_refs[j]
        for p, part in enumerate(PARTS):
            q_ref, kv_ref = out_refs[2 * p], out_refs[2 * p + 1]
            for i, h in enumerate(part):
                columns = slice(h * HEAD_DIM, (h + 1) * HEAD_DIM)
                q_ref[i * SET + j * ROWS : i * SET + (j + 1) * ROWS, :] = ref[0:ROWS, columns]
                for t in range(2):
                    base = (2 * i + t) * SET + j * ROWS
                    kv_ref[base : base + ROWS, :] = ref[(t + 1) * ROWS : (t + 2) * ROWS, columns]
        row = ref[3 * ROWS : 3 * ROWS + 16, 0:HEAD_DIM].astype(jnp.float32)
        out_refs[-1][j : j + 1, :] = row[0:1]


def attend_kernel(count, table_ref, *refs):
    together = 2 if count == 1 else 1
    q_refs, kv_refs = refs[:RING], refs[RING : 2 * RING]
    out_refs = refs[2 * RING : 3 * RING]
    q_all, k_all, v_all, o_all, v_turned, lse_ref = refs[3 * RING :]
    factor = jnp.float32(HEAD_DIM ** (-0.5) * LOG2E)
    limits = TILES * TILES
    q_place = [table_ref[limits + TILES + d] for d in range(RING)]
    k_place = [table_ref[limits + TILES + RING + d] for d in range(RING)]
    for h in range(count):
        for d in range(RING):
            for j in range(GROUP):
                rows = slice(h * SET + j * ROWS, h * SET + (j + 1) * ROWS)
                to = pl.multiple_of(j * RING * ROWS + q_place[d] * ROWS, ROWS)
                q_all[h, pl.ds(to, ROWS), :] = q_refs[d][rows, :]
                to = pl.multiple_of(j * RING * ROWS + k_place[d] * ROWS, ROWS)
                base = 2 * h * SET + j * ROWS
                k_all[h, pl.ds(to, ROWS), :] = kv_refs[d][base : base + ROWS, :]
                v_all[h, pl.ds(to, ROWS), :] = kv_refs[d][base + SET : base + SET + ROWS, :]

    for h in range(count):
        for i in range(TILES):
            rows = slice(i * TILE, (i + 1) * TILE)
            v_turned[h, :, rows] = v_all[h, rows, :].T

    def tiles(first, unused):
        picks = [first * together + t for t in range(together)]
        seen = [table_ref[limits + i] for i in picks]
        trips = functools.reduce(jnp.maximum, seen)
        chains = [(t, h) for t in range(together) for h in range(count)]
        starts = [pl.multiple_of(i * TILE, TILE) for i in picks]

        def step(g, carry):
            places = [
                [
                    pl.multiple_of(table_ref[i * TILES + g * STEP + u] * TILE, TILE)
                    for u in range(STEP)
                ]
                for i in picks
            ]
            scores = []
            for t, h in chains:
                scores.append(
                    lax.dot_general(
                        jnp.concatenate([k_all[h, pl.ds(at, TILE), :] for at in places[t]], axis=0),
                        q_all[h, pl.ds(starts[t], TILE), :],
                        (((1,), (1,)), ((), ())),
                        preferred_element_type=jnp.float32,
                    )
                )
            result = []
            for (t, h), score, (top, total, acc) in zip(chains, scores, carry):
                blocks = [
                    jnp.where(g * STEP + u < seen[t], score[u * TILE : (u + 1) * TILE], -1e30)
                    for u in range(STEP)
                ]
                largest = functools.reduce(jnp.maximum, blocks)
                new_top = jnp.maximum(top, jnp.max(largest, axis=0, keepdims=True))
                shrink = jnp.exp2((top - new_top) * factor)
                weights = [jnp.exp2((block - new_top) * factor) for block in blocks]
                added = functools.reduce(jnp.add, weights).reshape(TILE // 8, 8, TILE)
                total = total * shrink + jnp.sum(added, axis=0)
                weight = jnp.concatenate([w.astype(jnp.bfloat16) for w in weights], axis=0)
                acc = acc * shrink + jnp.dot(
                    jnp.concatenate([v_turned[h, :, pl.ds(at, TILE)] for at in places[t]], axis=1),
                    weight,
                    preferred_element_type=jnp.float32,
                )
                result.append((new_top, total, acc))
            return result

        empty = (
            jnp.full((1, TILE), -1e30, jnp.float32),
            jnp.zeros((8, TILE), jnp.float32),
            jnp.zeros((HEAD_DIM, TILE), jnp.float32),
        )
        final = lax.fori_loop(0, (trips + STEP - 1) // STEP, step, [empty] * len(chains))
        for (t, h), (top, total, acc) in zip(chains, final):
            total = jnp.sum(total, axis=0, keepdims=True)
            total = jnp.where(total > 0.0, total, 1.0)
            o_all[h, pl.ds(starts[t], TILE), :] = (acc * (1.0 / total)).T.astype(jnp.bfloat16)
            lse_ref[h, picks[t] % 2, pl.ds(picks[t] // 2, 1), :] = top * factor + jnp.log2(total)
        return unused

    lax.fori_loop(0, TILES // together, tiles, 0)
    for h in range(count):
        for d in range(RING):
            base = h * (SET + META)
            for j in range(GROUP):
                at = pl.multiple_of(j * RING * ROWS + q_place[d] * ROWS, ROWS)
                out_refs[d][base + j * ROWS : base + (j + 1) * ROWS, :] = o_all[
                    h, pl.ds(at, ROWS), :
                ]
            value = lse_ref[h, q_place[d] // 2]
            high = value.astype(jnp.bfloat16).astype(jnp.float32)
            middle = (value - high).astype(jnp.bfloat16).astype(jnp.float32)
            low = value - high - middle
            out_refs[d][base + SET : base + SET + META, :] = jnp.concatenate(
                [high, middle, low, jnp.zeros_like(low)], axis=0
            ).astype(jnp.bfloat16)


def attend(count, table, q, kv):
    all_rows = pltpu.VMEM((count, RING * SET, HEAD_DIM), jnp.bfloat16)
    return call(
        functools.partial(attend_kernel, count),
        [shape(count * (SET + META), HEAD_DIM)] * RING,
        [SMEM] + [VMEM] * (2 * RING),
        [all_rows] * 4
        + [
            pltpu.VMEM((count, HEAD_DIM, RING * SET), jnp.bfloat16),
            pltpu.VMEM((count, 2, GROUP, HEAD_DIM), jnp.float32),
        ],
    )(table, *q, *kv)


def combine_kernel(table_ref, *refs):
    out_refs = refs[-GROUP:]
    shift = table_ref[TILES * TILES + TILES] % 2 * ROWS
    lanes = lax.broadcasted_iota(jnp.int32, (ROWS, HEAD_DIM), 1)
    eye = lanes == lax.broadcasted_iota(jnp.int32, (ROWS, HEAD_DIM), 0) + shift
    for p, part in enumerate(PARTS):
        pieces = refs[p * RING : (p + 1) * RING]
        for i, h in enumerate(part):
            base = i * (SET + META)
            lse = []
            for ref in pieces:
                coded = ref[base + SET : base + SET + META, :].astype(jnp.float32)
                lse.append(coded[0:8] + coded[8:16] + coded[16:24])
            top = functools.reduce(jnp.maximum, lse)
            shares = [jnp.exp2(value - top) for value in lse]
            total = functools.reduce(jnp.add, shares)
            shares = [value / total for value in shares]
            for j in range(GROUP):
                mixed = jnp.zeros((ROWS, HEAD_DIM), jnp.float32)
                for ref, share in zip(pieces, shares):
                    column = jnp.sum(jnp.where(eye, share[j : j + 1], 0.0), axis=1, keepdims=True)
                    rows = ref[base + j * ROWS : base + (j + 1) * ROWS, :]
                    mixed = mixed + column * rows.astype(jnp.float32)
                out_refs[j][:, h * HEAD_DIM : (h + 1) * HEAD_DIM] = mixed.astype(jnp.bfloat16)


def finish_kernel(at_ref, level_ref, gates_ref, *refs):
    out_ref = refs[-1]
    for j in range(GROUP):
        columns = pl.ds(pl.multiple_of(at_ref[j] * WIDTH, HEAD_DIM), WIDTH)
        gate = gates_ref[pl.ds(level_ref[0], 1), columns]
        out_ref[:, columns] = (refs[j][...].astype(jnp.float32) * gate).astype(jnp.bfloat16)


def see_table(q_slots, k_slots, retiring, mask, places):
    names = jnp.arange(TILES, dtype=jnp.int32)
    q_order = (q_slots - retiring[0]) % SPANS
    k_order = (k_slots - retiring[0]) % SPANS
    slots = jnp.arange(SPANS, dtype=jnp.int32)
    picked = (k_slots[:, None] == slots[None, :]).astype(jnp.float32)
    masked = jnp.sum(mask[:, None, :SPANS] * picked[None], axis=-1) > 0.5
    older = k_order[None, :] < q_order[:, None]
    same = k_slots[None, :] == q_slots[:, None]
    sees = same | masked & older
    before = names[None, :] < names[:, None]
    rank = jnp.sum((sees[:, None, :] & before[None]).astype(jnp.int32), axis=-1)
    chosen = sees[:, None, :] & (rank[:, None, :] == names[None, :, None])
    listed = jnp.sum(jnp.where(chosen, names[None, None, :], 0), axis=-1)
    counts = jnp.sum(sees.astype(jnp.int32), axis=-1)
    return jnp.concatenate([listed.reshape(-1), counts, places])


def local(queries, keys, values, levels, retiring, block_mask, gates):
    span = lax.axis_index("span").astype(jnp.int32)
    token = lax.axis_index("tok").astype(jnp.int32)
    y, half, core = span // 4, span // 2 % 2, span % 2
    x, z = half * 2 + token // RING, token % RING
    hop = jnp.arange(GROUP, dtype=jnp.int32)
    target = (y + hop // 2) % 4 * 2 + (core ^ hop % 2)
    hops = [dict(dy=j // 2, core=j % 2) for j in range(GROUP)]
    backs = [dict(dy=-(j // 2), core=j % 2) for j in range(GROUP)]

    meta = jnp.pad(block_mask.astype(jnp.bfloat16), ((0, 15), (0, WIDTH - SPANS)))
    packed = call(
        pack_kernel,
        [shape(3 * ROWS + 16, WIDTH)] * GROUP,
        [SMEM, VMEM, VMEM, VMEM, VMEM],
    )(target, queries[0], keys[0], values[0], meta)
    shared = [packed[0]] + [moved(packed[j], **hops[j]) for j in range(1, GROUP)]

    shapes = []
    for part in PARTS:
        shapes += [shape(len(part) * SET, HEAD_DIM), shape(len(part) * 2 * SET, HEAD_DIM)]
    spread = call(
        spread_kernel, shapes + [shape(GROUP, HEAD_DIM, jnp.float32)], [VMEM] * GROUP
    )(*shared)

    tile = jnp.arange(TILES, dtype=jnp.int32)
    base = (y - tile // 4) % 4 * 4 + (core ^ tile // 2 % 2)
    wide_slots, near_slots = base + 2 * (tile % 2), base + 2 * half
    near_mask = jnp.repeat(spread[-1], 2, axis=0)
    far_mask = jnp.repeat(moved(spread[-1], dx=2), 2, axis=0)
    wide_mask = jnp.where((tile % 2 == half)[:, None], near_mask, far_mask)
    first = core == 0
    ring = jnp.arange(RING, dtype=jnp.int32)
    table = see_table(
        jnp.where(first, wide_slots, near_slots),
        jnp.where(first, near_slots, wide_slots),
        retiring,
        jnp.where(first, wide_mask, near_mask),
        jnp.concatenate(
            [(jnp.where(first, x, z) - ring) % RING, (jnp.where(first, z, x) - ring) % RING]
        ),
    )

    pieces = []
    for p, part in enumerate(PARTS):
        own_q, own_kv = spread[2 * p], spread[2 * p + 1]
        q = [own_q] + [moved(own_q, dx=d, swap=1) for d in range(1, RING)]
        kv = [own_kv] + [moved(own_kv, dz=d, swap=1) for d in range(1, RING)]
        parts = attend(len(part), table, q, kv)
        pieces += [parts[0]] + [moved(parts[d], dx=-d, swap=1) for d in range(1, RING)]

    mixed = call(
        combine_kernel, [shape(ROWS, WIDTH)] * GROUP, [SMEM] + [VMEM] * len(pieces)
    )(table, *pieces)
    returned = [mixed[0]] + [moved(mixed[j], **backs[j]) for j in range(1, GROUP)]
    result = call(finish_kernel, shape(ROWS, GROUP * WIDTH), [SMEM, SMEM] + [VMEM] * (GROUP + 1))(
        target, levels, gates, *returned
    )
    return result[None]


def solution(mesh):
    return jax.shard_map(
        local,
        mesh=mesh,
        in_specs=(
            P("span", "tok", None),
            P("span", "tok", None),
            P("span", "tok", None),
            P("span"),
            P(),
            P("span", None),
            P(),
        ),
        out_specs=P("span", "tok", None),
        check_vma=False,
    )
```

```python
import functools

import jax
import jax.numpy as jnp
from jax import lax
from jax.experimental import pallas as pl
from jax.experimental.pallas import tpu as pltpu
from jax.sharding import PartitionSpec as P


HEAD_DIM = 128
SPANS = 16
ROWS = 64
GROUP = 8
HEADS_DEV = 3
WIDTH = HEADS_DEV * HEAD_DIM
RING = 4
SET = GROUP * ROWS
META = 32
PARTS = ((0,), (1, 2))
TILE = 2 * ROWS
TILES = 16
STEP = 4
SUB = 2
LOG2E = 1.4426950408889634


BOTH = ("span", "tok")
VMEM = pl.BlockSpec(memory_space=pltpu.VMEM)
SMEM = pl.BlockSpec(memory_space=pltpu.SMEM)


def device_at(x, y, z, core):
    return (y * 4 + (x // 2) * 2 + core) * 8 + (x % 2) * 4 + z


def moved(array, dx=0, dy=0, dz=0, core=0, swap=0):
    pairs = []
    for x in range(4):
        for y in range(4):
            for z in range(4):
                for c in range(2):
                    mx, mz = (dz, dx) if swap and c else (dx, dz)
                    there = device_at((x + mx) % 4, (y + dy) % 4, (z + mz) % 4, c ^ core)
                    pairs.append((device_at(x, y, z, c), there))
    return lax.ppermute(array, BOTH, pairs)


def call(kernel, shapes, specs, scratch=()):
    return pl.pallas_call(
        kernel,
        out_shape=shapes,
        in_specs=specs,
        out_specs=jax.tree.map(lambda unused: VMEM, shapes),
        scratch_shapes=scratch,
    )


def shape(rows, columns, dtype=jnp.bfloat16):
    return jax.ShapeDtypeStruct((rows, columns), dtype)


def pack_kernel(at_ref, q_ref, k_ref, v_ref, meta_ref, *out_refs):
    for j in range(GROUP):
        columns = pl.ds(pl.multiple_of(at_ref[j] * WIDTH, HEAD_DIM), WIDTH)
        for i, ref in enumerate((q_ref, k_ref, v_ref)):
            out_refs[j][i * ROWS : (i + 1) * ROWS, :] = ref[:, columns]
        out_refs[j][3 * ROWS :, :] = meta_ref[...]


def spread_kernel(*refs):
    in_refs, out_refs = refs[:GROUP], refs[GROUP:]
    for j in range(GROUP):
        ref = in_refs[j]
        for p, part in enumerate(PARTS):
            q_ref, kv_ref = out_refs[2 * p], out_refs[2 * p + 1]
            for i, h in enumerate(part):
                columns = slice(h * HEAD_DIM, (h + 1) * HEAD_DIM)
                q_ref[i * SET + j * ROWS : i * SET + (j + 1) * ROWS, :] = ref[0:ROWS, columns]
                for t in range(2):
                    base = (2 * i + t) * SET + j * ROWS
                    kv_ref[base : base + ROWS, :] = ref[(t + 1) * ROWS : (t + 2) * ROWS, columns]
        row = ref[3 * ROWS : 3 * ROWS + 16, 0:HEAD_DIM].astype(jnp.float32)
        out_refs[-1][j : j + 1, :] = row[0:1]


def together_in(count):
    return 2 if count == 1 else 1


def attend_kernel(count, table_ref, *refs):
    together = together_in(count)
    q_refs, kv_refs = refs[:RING], refs[RING : 2 * RING]
    out_refs = refs[2 * RING : 3 * RING]
    q_all, k_all, v_all, o_all, v_turned, score_ref, lse_ref, sems = refs[3 * RING :]
    factor = jnp.float32(HEAD_DIM ** (-0.5) * LOG2E)

    def rows_of(ref, h, i):
        return ref[h, i // 2, pl.ds(i % 2 * 2, 2)].reshape(TILE, HEAD_DIM)

    limits = TILES * TILES
    q_place = [table_ref[limits + TILES + d] for d in range(RING)]
    k_place = [table_ref[limits + TILES + RING + d] for d in range(RING)]
    copies = []
    for h in range(count):
        for d in range(RING):
            for n, (source, target, place) in enumerate(
                (
                    (q_refs[d].at[h], q_all, q_place[d]),
                    (kv_refs[d].at[h, 0], k_all, k_place[d]),
                    (kv_refs[d].at[h, 1], v_all, k_place[d]),
                )
            ):
                copy = pltpu.make_async_copy(
                    source, target.at[h, :, place], sems.at[(h * RING + d) * 3 + n]
                )
                copy.start()
                copies.append(copy)
    for copy in copies:
        copy.wait()
    for h in range(count):
        for i in range(TILES):
            rows = slice(i * TILE, (i + 1) * TILE)
            v_turned[h, :, rows] = rows_of(v_all, h, i).T

    def tiles(first, unused):
        picks = [first * together + t for t in range(together)]
        seen = [table_ref[limits + i] for i in picks]
        trips = functools.reduce(jnp.maximum, seen)
        chains = [(t, h) for t in range(together) for h in range(count)]
        starts = [pl.multiple_of(i * TILE, TILE) for i in picks]

        def fill(g):
            for c, (t, h) in enumerate(chains):
                rows = [rows_of(k_all, h, place(t, g, u)) for u in range(STEP)]
                score_ref[c] = lax.dot_general(
                    jnp.concatenate(rows, axis=0),
                    rows_of(q_all, h, picks[t]),
                    (((1,), (1,)), ((), ())),
                    preferred_element_type=jnp.float32,
                )

        def place(t, g, u):
            return table_ref[picks[t] * TILES + g * STEP + u]

        fill(0)

        def step(g, carry):
            parts = [range(at, at + SUB) for at in range(0, STEP, SUB)]
            scores = [score_ref[c] for c in range(len(chains))]
            fill(jnp.minimum(g + 1, TILES // STEP - 1))
            result = list(carry)
            for part in parts:
                for c, (t, h) in enumerate(chains):
                    top, total, acc = result[c]
                    score = scores[c][part[0] * TILE : (part[-1] + 1) * TILE]
                    blocks = []
                    for n, u in enumerate(part):
                        block = score[n * TILE : (n + 1) * TILE]
                        blocks.append(jnp.where(g * STEP + u < seen[t], block, -1e30))
                    largest = functools.reduce(jnp.maximum, blocks)
                    new_top = jnp.maximum(top, jnp.max(largest, axis=0, keepdims=True))
                    shrink = jnp.exp2((top - new_top) * factor)
                    weights = [jnp.exp2((block - new_top) * factor) for block in blocks]
                    added = functools.reduce(jnp.add, weights).reshape(TILE // 8, 8, TILE)
                    total = total * shrink + jnp.sum(added, axis=0)
                    weight = jnp.concatenate([w.astype(jnp.bfloat16) for w in weights], axis=0)
                    columns = [v_turned[h, :, pl.ds(pl.multiple_of(place(t, g, u) * TILE, TILE), TILE)] for u in part]
                    acc = acc * shrink + jnp.dot(
                        jnp.concatenate(columns, axis=1),
                        weight,
                        preferred_element_type=jnp.float32,
                    )
                    result[c] = (new_top, total, acc)
            return result

        empty = (
            jnp.full((1, TILE), -1e30, jnp.float32),
            jnp.zeros((8, TILE), jnp.float32),
            jnp.zeros((HEAD_DIM, TILE), jnp.float32),
        )
        final = lax.fori_loop(0, (trips + STEP - 1) // STEP, step, [empty] * len(chains))
        for (t, h), (top, total, acc) in zip(chains, final):
            total = jnp.sum(total, axis=0, keepdims=True)
            total = jnp.where(total > 0.0, total, 1.0)
            o_all[h, pl.ds(starts[t], TILE), :] = (acc * (1.0 / total)).T.astype(jnp.bfloat16)
            lse_ref[h, picks[t] % 2, pl.ds(picks[t] // 2, 1), :] = top * factor + jnp.log2(total)
        return unused

    lax.fori_loop(0, TILES // together, tiles, 0)
    for h in range(count):
        for d in range(RING):
            base = h * (SET + META)
            for j in range(GROUP):
                at = pl.multiple_of(j * RING * ROWS + q_place[d] * ROWS, ROWS)
                out_refs[d][base + j * ROWS : base + (j + 1) * ROWS, :] = o_all[
                    h, pl.ds(at, ROWS), :
                ]
            value = lse_ref[h, q_place[d] // 2]
            high = value.astype(jnp.bfloat16).astype(jnp.float32)
            middle = (value - high).astype(jnp.bfloat16).astype(jnp.float32)
            low = value - high - middle
            out_refs[d][base + SET : base + SET + META, :] = jnp.concatenate(
                [high, middle, low, jnp.zeros_like(low)], axis=0
            ).astype(jnp.bfloat16)


def attend(count, table, q, kv):
    q = [piece.reshape(count, GROUP, ROWS, HEAD_DIM) for piece in q]
    kv = [piece.reshape(count, 2, GROUP, ROWS, HEAD_DIM) for piece in kv]
    pieces = pltpu.VMEM((count, GROUP, RING, ROWS, HEAD_DIM), jnp.bfloat16)
    return call(
        functools.partial(attend_kernel, count),
        [shape(count * (SET + META), HEAD_DIM)] * RING,
        [SMEM] + [pl.BlockSpec(memory_space=pl.ANY)] * (2 * RING),
        [pieces] * 3
        + [
            pltpu.VMEM((count, RING * SET, HEAD_DIM), jnp.bfloat16),
            pltpu.VMEM((count, HEAD_DIM, RING * SET), jnp.bfloat16),
            pltpu.VMEM((count * together_in(count), STEP * TILE, TILE), jnp.float32),
            pltpu.VMEM((count, 2, GROUP, HEAD_DIM), jnp.float32),
            pltpu.SemaphoreType.DMA((count * RING * 3,)),
        ],
    )(table, *q, *kv)


def combine_kernel(table_ref, *refs):
    out_refs = refs[-GROUP:]
    shift = table_ref[TILES * TILES + TILES] % 2 * ROWS
    lanes = lax.broadcasted_iota(jnp.int32, (ROWS, HEAD_DIM), 1)
    eye = lanes == lax.broadcasted_iota(jnp.int32, (ROWS, HEAD_DIM), 0) + shift
    for p, part in enumerate(PARTS):
        pieces = refs[p * RING : (p + 1) * RING]
        for i, h in enumerate(part):
            base = i * (SET + META)
            lse = []
            for ref in pieces:
                coded = ref[base + SET : base + SET + META, :].astype(jnp.float32)
                lse.append(coded[0:8] + coded[8:16] + coded[16:24])
            top = functools.reduce(jnp.maximum, lse)
            shares = [jnp.exp2(value - top) for value in lse]
            total = functools.reduce(jnp.add, shares)
            shares = [value / total for value in shares]
            for j in range(GROUP):
                mixed = jnp.zeros((ROWS, HEAD_DIM), jnp.float32)
                for ref, share in zip(pieces, shares):
                    column = jnp.sum(jnp.where(eye, share[j : j + 1], 0.0), axis=1, keepdims=True)
                    rows = ref[base + j * ROWS : base + (j + 1) * ROWS, :]
                    mixed = mixed + column * rows.astype(jnp.float32)
                out_refs[j][:, h * HEAD_DIM : (h + 1) * HEAD_DIM] = mixed.astype(jnp.bfloat16)


def finish_kernel(at_ref, level_ref, gates_ref, *refs):
    out_ref = refs[-1]
    for j in range(GROUP):
        columns = pl.ds(pl.multiple_of(at_ref[j] * WIDTH, HEAD_DIM), WIDTH)
        gate = gates_ref[pl.ds(level_ref[0], 1), columns]
        out_ref[:, columns] = (refs[j][...].astype(jnp.float32) * gate).astype(jnp.bfloat16)


def see_table(q_slots, k_slots, retiring, mask, places):
    names = jnp.arange(TILES, dtype=jnp.int32)
    q_order = (q_slots - retiring[0]) % SPANS
    k_order = (k_slots - retiring[0]) % SPANS
    slots = jnp.arange(SPANS, dtype=jnp.int32)
    picked = (k_slots[:, None] == slots[None, :]).astype(jnp.float32)
    masked = jnp.sum(mask[:, None, :SPANS] * picked[None], axis=-1) > 0.5
    older = k_order[None, :] < q_order[:, None]
    same = k_slots[None, :] == q_slots[:, None]
    sees = same | masked & older
    before = names[None, :] < names[:, None]
    rank = jnp.sum((sees[:, None, :] & before[None]).astype(jnp.int32), axis=-1)
    chosen = sees[:, None, :] & (rank[:, None, :] == names[None, :, None])
    listed = jnp.sum(jnp.where(chosen, names[None, None, :], 0), axis=-1)
    counts = jnp.sum(sees.astype(jnp.int32), axis=-1)
    return jnp.concatenate([listed.reshape(-1), counts, places])


def local(queries, keys, values, levels, retiring, block_mask, gates):
    span = lax.axis_index("span").astype(jnp.int32)
    token = lax.axis_index("tok").astype(jnp.int32)
    y, half, core = span // 4, span // 2 % 2, span % 2
    x, z = half * 2 + token // RING, token % RING
    hop = jnp.arange(GROUP, dtype=jnp.int32)
    target = (y + hop // 2) % 4 * 2 + (core ^ hop % 2)
    hops = [dict(dy=j // 2, core=j % 2) for j in range(GROUP)]
    backs = [dict(dy=-(j // 2), core=j % 2) for j in range(GROUP)]

    meta = jnp.pad(block_mask.astype(jnp.bfloat16), ((0, 15), (0, WIDTH - SPANS)))
    packed = call(
        pack_kernel,
        [shape(3 * ROWS + 16, WIDTH)] * GROUP,
        [SMEM, VMEM, VMEM, VMEM, VMEM],
    )(target, queries[0], keys[0], values[0], meta)
    shared = [packed[0]] + [moved(packed[j], **hops[j]) for j in range(1, GROUP)]

    shapes = []
    for part in PARTS:
        shapes += [shape(len(part) * SET, HEAD_DIM), shape(len(part) * 2 * SET, HEAD_DIM)]
    spread = call(
        spread_kernel, shapes + [shape(GROUP, HEAD_DIM, jnp.float32)], [VMEM] * GROUP
    )(*shared)

    tile = jnp.arange(TILES, dtype=jnp.int32)
    base = (y - tile // 4) % 4 * 4 + (core ^ tile // 2 % 2)
    wide_slots, near_slots = base + 2 * (tile % 2), base + 2 * half
    near_mask = jnp.repeat(spread[-1], 2, axis=0)
    far_mask = jnp.repeat(moved(spread[-1], dx=2), 2, axis=0)
    wide_mask = jnp.where((tile % 2 == half)[:, None], near_mask, far_mask)
    first = core == 0
    ring = jnp.arange(RING, dtype=jnp.int32)
    table = see_table(
        jnp.where(first, wide_slots, near_slots),
        jnp.where(first, near_slots, wide_slots),
        retiring,
        jnp.where(first, wide_mask, near_mask),
        jnp.concatenate(
            [(jnp.where(first, x, z) - ring) % RING, (jnp.where(first, z, x) - ring) % RING]
        ),
    )

    pieces = []
    for p, part in enumerate(PARTS):
        own_q, own_kv = spread[2 * p], spread[2 * p + 1]
        q, kv = [own_q], [own_kv]
        for d in range(1, RING):
            kv.append(moved(own_kv, dz=d, swap=1))
        for d in range(1, RING):
            q.append(moved(own_q, dx=d, swap=1))
        parts = attend(len(part), table, q, kv)
        pieces.append(parts[0])
        for d in range(1, RING):
            pieces.append(moved(parts[d], dx=-d, swap=1))

    mixed = call(
        combine_kernel, [shape(ROWS, WIDTH)] * GROUP, [SMEM] + [VMEM] * len(pieces)
    )(table, *pieces)
    returned = [mixed[0]] + [moved(mixed[j], **backs[j]) for j in range(1, GROUP)]
    result = call(finish_kernel, shape(ROWS, GROUP * WIDTH), [SMEM, SMEM] + [VMEM] * (GROUP + 1))(
        target, levels, gates, *returned
    )
    return result[None]


def solution(mesh):
    return jax.shard_map(
        local,
        mesh=mesh,
        in_specs=(
            P("span", "tok", None),
            P("span", "tok", None),
            P("span", "tok", None),
            P("span"),
            P(),
            P("span", None),
            P(),
        ),
        out_specs=P("span", "tok", None),
        check_vma=False,
    )
```

```python
import functools

import jax
import jax.numpy as jnp
from jax import lax
from jax.experimental import pallas as pl
from jax.experimental.pallas import tpu as pltpu
from jax.sharding import PartitionSpec as P


HEAD_DIM = 128
SPANS = 16
ROWS = 64
GROUP = 8
HEADS_DEV = 3
WIDTH = HEADS_DEV * HEAD_DIM
RING = 4
SET = GROUP * ROWS
META = 32
PARTS = ((0,), (1, 2))
TILE = 2 * ROWS
TILES = 16
STEP = 4
SUB = 2
LOG2E = 1.4426950408889634


BOTH = ("span", "tok")
VMEM = pl.BlockSpec(memory_space=pltpu.VMEM)
SMEM = pl.BlockSpec(memory_space=pltpu.SMEM)
ANY = pl.BlockSpec(memory_space=pl.ANY)


def device_at(x, y, z, core):
    return (y * 4 + (x // 2) * 2 + core) * 8 + (x % 2) * 4 + z


def moved(array, dx=0, dy=0, dz=0, core=0, swap=0):
    pairs = []
    for x in range(4):
        for y in range(4):
            for z in range(4):
                for c in range(2):
                    mx, mz = (dz, dx) if swap and c else (dx, dz)
                    there = device_at((x + mx) % 4, (y + dy) % 4, (z + mz) % 4, c ^ core)
                    pairs.append((device_at(x, y, z, c), there))
    return lax.ppermute(array, BOTH, pairs)


def call(kernel, shapes, specs, scratch=()):
    return pl.pallas_call(
        kernel,
        out_shape=shapes,
        in_specs=specs,
        out_specs=jax.tree.map(lambda unused: VMEM, shapes),
        scratch_shapes=scratch,
    )


def shape(rows, columns, dtype=jnp.bfloat16):
    return jax.ShapeDtypeStruct((rows, columns), dtype)


def pack_kernel(at_ref, q_ref, k_ref, v_ref, meta_ref, *out_refs):
    for j in range(GROUP):
        columns = pl.ds(pl.multiple_of(at_ref[j] * WIDTH, HEAD_DIM), WIDTH)
        for i, ref in enumerate((q_ref, k_ref, v_ref)):
            out_refs[j][i * ROWS : (i + 1) * ROWS, :] = ref[:, columns]
        out_refs[j][3 * ROWS :, :] = meta_ref[...]


def spread_kernel(*refs):
    in_refs, out_refs, sems = refs[:GROUP], refs[GROUP:-1], refs[-1]
    copies = []

    def send(source, target):
        copy = pltpu.make_async_copy(source, target, sems.at[len(copies)])
        copy.start()
        copies.append(copy)

    for p, part in enumerate(PARTS):
        q_ref, kv_ref = out_refs[2 * p], out_refs[2 * p + 1]
        for i, h in enumerate(part):
            columns = pl.ds(h * HEAD_DIM, HEAD_DIM)
            for j, ref in enumerate(in_refs):
                send(ref.at[pl.ds(0, ROWS), columns], q_ref.at[i, j])
                for t in range(2):
                    send(ref.at[pl.ds((t + 1) * ROWS, ROWS), columns], kv_ref.at[i, t, j])
    for j, ref in enumerate(in_refs):
        send(ref.at[pl.ds(3 * ROWS, 16), pl.ds(0, HEAD_DIM)], out_refs[-1].at[j])
    for copy in copies:
        copy.wait()


def fetched(kernel, small, count, *refs):
    sems, held = refs[-1], refs[-1 - count : -1]
    copies = [
        pltpu.make_async_copy(refs[small + n], held[n], sems.at[n]) for n in range(count)
    ]
    for copy in copies:
        copy.start()
    for copy in copies:
        copy.wait()
    kernel(*refs[:small], *held, *refs[small + count : -1 - count])


def call_fetched(kernel, shapes, specs, ready, pieces):
    count = len(pieces)
    return pl.pallas_call(
        functools.partial(fetched, kernel, len(ready), count),
        out_shape=shapes,
        in_specs=specs + [ANY] * count,
        out_specs=jax.tree.map(lambda unused: VMEM, shapes),
        scratch_shapes=[pltpu.VMEM(piece.shape, piece.dtype) for piece in pieces]
        + [pltpu.SemaphoreType.DMA((count,))],
    )(*ready, *pieces)


def together_in(count):
    return 2 if count == 1 else 1


def attend_kernel(count, table_ref, *refs):
    together = together_in(count)
    q_refs, kv_refs = refs[:RING], refs[RING : 2 * RING]
    out_refs = refs[2 * RING : 3 * RING]
    q_all, k_all, v_all, o_all, v_turned, score_ref, lse_ref, sems = refs[3 * RING :]
    factor = jnp.float32(HEAD_DIM ** (-0.5) * LOG2E)

    def rows_of(ref, h, i):
        return ref[h, i // 2, pl.ds(i % 2 * 2, 2)].reshape(TILE, HEAD_DIM)

    limits = TILES * TILES
    q_place = [table_ref[limits + TILES + d] for d in range(RING)]
    k_place = [table_ref[limits + TILES + RING + d] for d in range(RING)]
    copies = []
    for h in range(count):
        for d in range(RING):
            for n, (source, target, place) in enumerate(
                (
                    (q_refs[d].at[h], q_all, q_place[d]),
                    (kv_refs[d].at[h, 0], k_all, k_place[d]),
                    (kv_refs[d].at[h, 1], v_all, k_place[d]),
                )
            ):
                copy = pltpu.make_async_copy(
                    source, target.at[h, :, place], sems.at[(h * RING + d) * 3 + n]
                )
                copy.start()
                copies.append(copy)
    for copy in copies:
        copy.wait()
    for h in range(count):
        for i in range(TILES):
            rows = slice(i * TILE, (i + 1) * TILE)
            v_turned[h, :, rows] = rows_of(v_all, h, i).T

    chains = [(t, h) for t in range(together) for h in range(count)]

    def trips_of(first):
        seen = [table_ref[limits + first * together + t] for t in range(together)]
        return jnp.maximum((functools.reduce(jnp.maximum, seen) + STEP - 1) // STEP, 1)

    def fill(first, g):
        for c, (t, h) in enumerate(chains):
            pick = first * together + t
            at = pick * TILES + g * STEP
            rows = [rows_of(k_all, h, table_ref[at + u]) for u in range(STEP)]
            score_ref[c] = lax.dot_general(
                jnp.concatenate(rows, axis=0),
                rows_of(q_all, h, pick),
                (((1,), (1,)), ((), ())),
                preferred_element_type=jnp.float32,
            )

    def tiles(first, unused):
        picks = [first * together + t for t in range(together)]
        seen = [table_ref[limits + i] for i in picks]
        trips = trips_of(first)
        starts = [pl.multiple_of(i * TILE, TILE) for i in picks]

        def place(t, g, u):
            return table_ref[picks[t] * TILES + g * STEP + u]

        def step(g, carry):
            parts = [range(at, at + SUB) for at in range(0, STEP, SUB)]
            scores = [score_ref[c] for c in range(len(chains))]
            last = (g + 1 >= trips).astype(jnp.int32)
            fill(jnp.minimum(first + last, TILES // together - 1), (1 - last) * (g + 1))
            result = list(carry)
            for part in parts:
                for c, (t, h) in enumerate(chains):
                    top, total, acc = result[c]
                    score = scores[c][part[0] * TILE : (part[-1] + 1) * TILE]
                    blocks = []
                    for n, u in enumerate(part):
                        block = score[n * TILE : (n + 1) * TILE]
                        blocks.append(jnp.where(g * STEP + u < seen[t], block, -1e30))
                    largest = functools.reduce(jnp.maximum, blocks)
                    new_top = jnp.maximum(top, jnp.max(largest, axis=0, keepdims=True))
                    shrink = jnp.exp2((top - new_top) * factor)
                    weights = [jnp.exp2((block - new_top) * factor) for block in blocks]
                    added = functools.reduce(jnp.add, weights).reshape(TILE // 8, 8, TILE)
                    total = total * shrink + jnp.sum(added, axis=0)
                    weight = jnp.concatenate([w.astype(jnp.bfloat16) for w in weights], axis=0)
                    ats = [pl.multiple_of(place(t, g, u) * TILE, TILE) for u in part]
                    columns = [v_turned[h, :, pl.ds(at, TILE)] for at in ats]
                    acc = acc * shrink + jnp.dot(
                        jnp.concatenate(columns, axis=1),
                        weight,
                        preferred_element_type=jnp.float32,
                    )
                    result[c] = (new_top, total, acc)
            return result

        empty = (
            jnp.full((1, TILE), -1e30, jnp.float32),
            jnp.zeros((8, TILE), jnp.float32),
            jnp.zeros((HEAD_DIM, TILE), jnp.float32),
        )
        final = lax.fori_loop(0, trips, step, [empty] * len(chains))
        for (t, h), (top, total, acc) in zip(chains, final):
            total = jnp.sum(total, axis=0, keepdims=True)
            total = jnp.where(total > 0.0, total, 1.0)
            o_all[h, pl.ds(starts[t], TILE), :] = (acc * (1.0 / total)).T.astype(jnp.bfloat16)
            lse_ref[h, picks[t] % 2, pl.ds(picks[t] // 2, 1), :] = top * factor + jnp.log2(total)
        return unused

    fill(0, 0)
    lax.fori_loop(0, TILES // together, tiles, 0)
    for h in range(count):
        for d in range(RING):
            base = h * (SET + META)
            for j in range(GROUP):
                at = pl.multiple_of(j * RING * ROWS + q_place[d] * ROWS, ROWS)
                out_refs[d][base + j * ROWS : base + (j + 1) * ROWS, :] = o_all[
                    h, pl.ds(at, ROWS), :
                ]
            value = lse_ref[h, q_place[d] // 2]
            high = value.astype(jnp.bfloat16).astype(jnp.float32)
            middle = (value - high).astype(jnp.bfloat16).astype(jnp.float32)
            low = value - high - middle
            out_refs[d][base + SET : base + SET + META, :] = jnp.concatenate(
                [high, middle, low, jnp.zeros_like(low)], axis=0
            ).astype(jnp.bfloat16)


def attend(count, table, q, kv):
    pieces = pltpu.VMEM((count, GROUP, RING, ROWS, HEAD_DIM), jnp.bfloat16)
    return call(
        functools.partial(attend_kernel, count),
        [shape(count * (SET + META), HEAD_DIM)] * RING,
        [SMEM] + [ANY] * (2 * RING),
        [pieces] * 3
        + [
            pltpu.VMEM((count, RING * SET, HEAD_DIM), jnp.bfloat16),
            pltpu.VMEM((count, HEAD_DIM, RING * SET), jnp.bfloat16),
            pltpu.VMEM((count * together_in(count), STEP * TILE, TILE), jnp.float32),
            pltpu.VMEM((count, 2, GROUP, HEAD_DIM), jnp.float32),
            pltpu.SemaphoreType.DMA((count * RING * 3,)),
        ],
    )(table, *q, *kv)


def combine_kernel(table_ref, *refs):
    out_refs = refs[-GROUP:]
    shift = table_ref[TILES * TILES + TILES] % 2 * ROWS
    lanes = lax.broadcasted_iota(jnp.int32, (ROWS, HEAD_DIM), 1)
    eye = lanes == lax.broadcasted_iota(jnp.int32, (ROWS, HEAD_DIM), 0) + shift
    for p, part in enumerate(PARTS):
        pieces = refs[p * RING : (p + 1) * RING]
        for i, h in enumerate(part):
            base = i * (SET + META)
            lse = []
            for ref in pieces:
                coded = ref[base + SET : base + SET + META, :].astype(jnp.float32)
                lse.append(coded[0:8] + coded[8:16] + coded[16:24])
            top = functools.reduce(jnp.maximum, lse)
            shares = [jnp.exp2(value - top) for value in lse]
            total = functools.reduce(jnp.add, shares)
            shares = [value / total for value in shares]
            for j in range(GROUP):
                mixed = jnp.zeros((ROWS, HEAD_DIM), jnp.float32)
                for ref, share in zip(pieces, shares):
                    column = jnp.sum(jnp.where(eye, share[j : j + 1], 0.0), axis=1, keepdims=True)
                    rows = ref[base + j * ROWS : base + (j + 1) * ROWS, :]
                    mixed = mixed + column * rows.astype(jnp.float32)
                out_refs[j][:, h * HEAD_DIM : (h + 1) * HEAD_DIM] = mixed.astype(jnp.bfloat16)


def finish_kernel(at_ref, level_ref, gates_ref, *refs):
    out_ref = refs[-1]
    for j in range(GROUP):
        columns = pl.ds(pl.multiple_of(at_ref[j] * WIDTH, HEAD_DIM), WIDTH)
        gate = gates_ref[pl.ds(level_ref[0], 1), columns]
        out_ref[:, columns] = (refs[j][...].astype(jnp.float32) * gate).astype(jnp.bfloat16)


def see_table(q_slots, k_slots, retiring, mask, places):
    names = jnp.arange(TILES, dtype=jnp.int32)
    q_order = (q_slots - retiring[0]) % SPANS
    k_order = (k_slots - retiring[0]) % SPANS
    slots = jnp.arange(SPANS, dtype=jnp.int32)
    picked = (k_slots[:, None] == slots[None, :]).astype(jnp.float32)
    masked = jnp.sum(mask[:, None, :SPANS] * picked[None], axis=-1) > 0.5
    older = k_order[None, :] < q_order[:, None]
    same = k_slots[None, :] == q_slots[:, None]
    sees = same | masked & older
    before = names[None, :] < names[:, None]
    rank = jnp.sum((sees[:, None, :] & before[None]).astype(jnp.int32), axis=-1)
    chosen = sees[:, None, :] & (rank[:, None, :] == names[None, :, None])
    listed = jnp.sum(jnp.where(chosen, names[None, None, :], 0), axis=-1)
    counts = jnp.sum(sees.astype(jnp.int32), axis=-1)
    return jnp.concatenate([listed.reshape(-1), counts, places])


def local(queries, keys, values, levels, retiring, block_mask, gates):
    span = lax.axis_index("span").astype(jnp.int32)
    token = lax.axis_index("tok").astype(jnp.int32)
    y, half, core = span // 4, span // 2 % 2, span % 2
    x, z = half * 2 + token // RING, token % RING
    hop = jnp.arange(GROUP, dtype=jnp.int32)
    target = (y + hop // 2) % 4 * 2 + (core ^ hop % 2)
    hops = [dict(dy=j // 2, core=j % 2) for j in range(GROUP)]
    backs = [dict(dy=-(j // 2), core=j % 2) for j in range(GROUP)]

    meta = jnp.pad(block_mask.astype(jnp.bfloat16), ((0, 15), (0, WIDTH - SPANS)))
    packed = call(
        pack_kernel,
        [shape(3 * ROWS + 16, WIDTH)] * GROUP,
        [SMEM, VMEM, VMEM, VMEM, VMEM],
    )(target, queries[0], keys[0], values[0], meta)
    shared = [packed[0]] + [moved(packed[j], **hops[j]) for j in range(1, GROUP)]

    shapes = []
    for part in PARTS:
        shapes.append((len(part), GROUP, ROWS, HEAD_DIM))
        shapes.append((len(part), 2, GROUP, ROWS, HEAD_DIM))
    shapes = [jax.ShapeDtypeStruct(dims, jnp.bfloat16) for dims in shapes + [(GROUP, 16, HEAD_DIM)]]
    spread = pl.pallas_call(
        spread_kernel,
        out_shape=shapes,
        in_specs=[ANY] * GROUP,
        out_specs=[ANY] * len(shapes),
        scratch_shapes=[pltpu.SemaphoreType.DMA((3 * HEADS_DEV * GROUP + GROUP,))],
    )(*shared)

    tile = jnp.arange(TILES, dtype=jnp.int32)
    base = (y - tile // 4) % 4 * 4 + (core ^ tile // 2 % 2)
    wide_slots, near_slots = base + 2 * (tile % 2), base + 2 * half
    near_mask, far_mask = [
        jnp.repeat(rows[:, 0, :SPANS].astype(jnp.float32), 2, axis=0)
        for rows in (spread[-1], moved(spread[-1], dx=2))
    ]
    wide_mask = jnp.where((tile % 2 == half)[:, None], near_mask, far_mask)
    first = core == 0
    ring = jnp.arange(RING, dtype=jnp.int32)
    table = see_table(
        jnp.where(first, wide_slots, near_slots),
        jnp.where(first, near_slots, wide_slots),
        retiring,
        jnp.where(first, wide_mask, near_mask),
        jnp.concatenate(
            [(jnp.where(first, x, z) - ring) % RING, (jnp.where(first, z, x) - ring) % RING]
        ),
    )

    pieces = []
    for p, part in enumerate(PARTS):
        own_q, own_kv = spread[2 * p], spread[2 * p + 1]
        q, kv = [own_q], [own_kv]
        for d in range(1, RING):
            kv.append(moved(own_kv, dz=d, swap=1))
        for d in range(1, RING):
            q.append(moved(own_q, dx=d, swap=1))
        parts = attend(len(part), table, q, kv)
        pieces.append(parts[0])
        for d in range(1, RING):
            pieces.append(moved(parts[d], dx=-d, swap=1))

    mixed = call_fetched(combine_kernel, [shape(ROWS, WIDTH)] * GROUP, [SMEM], [table], pieces)
    returned = [mixed[0]] + [moved(mixed[j], **backs[j]) for j in range(1, GROUP)]
    result = call_fetched(
        finish_kernel,
        shape(ROWS, GROUP * WIDTH),
        [SMEM, SMEM, VMEM],
        [target, levels, gates],
        returned,
    )
    return result[None]


def solution(mesh):
    return jax.shard_map(
        local,
        mesh=mesh,
        in_specs=(
            P("span", "tok", None),
            P("span", "tok", None),
            P("span", "tok", None),
            P("span"),
            P(),
            P("span", None),
            P(),
        ),
        out_specs=P("span", "tok", None),
        check_vma=False,
    )
```

```python
import functools

import jax
import jax.numpy as jnp
from jax import lax
from jax.experimental import pallas as pl
from jax.experimental.pallas import tpu as pltpu
from jax.sharding import PartitionSpec as P


HEAD_DIM = 128
SPANS = 16
ROWS = 64
GROUP = 8
HEADS_DEV = 3
WIDTH = HEADS_DEV * HEAD_DIM
RING = 4
SET = GROUP * ROWS
META = 32
PARTS = ((0, 1), (2,))
TILE = 2 * ROWS
TILES = 16
STEP = 4
SUB = 2
LOG2E = 1.4426950408889634


BOTH = ("span", "tok")
VMEM = pl.BlockSpec(memory_space=pltpu.VMEM)
SMEM = pl.BlockSpec(memory_space=pltpu.SMEM)


def device_at(x, y, z, core):
    return (y * 4 + (x // 2) * 2 + core) * 8 + (x % 2) * 4 + z


def moved(array, dx=0, dy=0, dz=0, core=0, swap=0):
    pairs = []
    for x in range(4):
        for y in range(4):
            for z in range(4):
                for c in range(2):
                    mx, mz = (dz, dx) if swap and c else (dx, dz)
                    there = device_at((x + mx) % 4, (y + dy) % 4, (z + mz) % 4, c ^ core)
                    pairs.append((device_at(x, y, z, c), there))
    return lax.ppermute(array, BOTH, pairs)


def call(kernel, shapes, specs, scratch=()):
    return pl.pallas_call(
        kernel,
        out_shape=shapes,
        in_specs=specs,
        out_specs=jax.tree.map(lambda unused: VMEM, shapes),
        scratch_shapes=scratch,
    )


def shape(rows, columns, dtype=jnp.bfloat16):
    return jax.ShapeDtypeStruct((rows, columns), dtype)


def pack_kernel(at_ref, q_ref, k_ref, v_ref, meta_ref, *out_refs):
    for j in range(GROUP):
        columns = pl.ds(pl.multiple_of(at_ref[j] * WIDTH, HEAD_DIM), WIDTH)
        for i, ref in enumerate((q_ref, k_ref, v_ref)):
            out_refs[j][i * ROWS : (i + 1) * ROWS, :] = ref[:, columns]
        out_refs[j][3 * ROWS :, :] = meta_ref[...]


def spread_kernel(*refs):
    in_refs, out_refs = refs[:GROUP], refs[GROUP:]
    for j in range(GROUP):
        ref = in_refs[j]
        for p, part in enumerate(PARTS):
            q_ref, kv_ref = out_refs[2 * p], out_refs[2 * p + 1]
            for i, h in enumerate(part):
                columns = slice(h * HEAD_DIM, (h + 1) * HEAD_DIM)
                q_ref[i * SET + j * ROWS : i * SET + (j + 1) * ROWS, :] = ref[0:ROWS, columns]
                for t in range(2):
                    base = (2 * i + t) * SET + j * ROWS
                    kv_ref[base : base + ROWS, :] = ref[(t + 1) * ROWS : (t + 2) * ROWS, columns]
        row = ref[3 * ROWS : 3 * ROWS + 16, 0:HEAD_DIM].astype(jnp.float32)
        out_refs[-1][j : j + 1, :] = row[0:1]


def together_in(count):
    return 2 if count == 1 else 1


def attend_kernel(count, table_ref, *refs):
    together = together_in(count)
    q_refs, kv_refs = refs[:RING], refs[RING : 2 * RING]
    out_refs = refs[2 * RING : 3 * RING]
    q_all, k_all, v_all, o_all, v_turned, score_ref, lse_ref, sems = refs[3 * RING :]
    factor = jnp.float32(HEAD_DIM ** (-0.5) * LOG2E)

    def rows_of(ref, h, i):
        return ref[h, i // 2, pl.ds(i % 2 * 2, 2)].reshape(TILE, HEAD_DIM)

    limits = TILES * TILES
    q_place = [table_ref[limits + TILES + d] for d in range(RING)]
    k_place = [table_ref[limits + TILES + RING + d] for d in range(RING)]
    copies = []
    for h in range(count):
        for d in range(RING):
            for n, (source, target, place) in enumerate(
                (
                    (q_refs[d].at[h], q_all, q_place[d]),
                    (kv_refs[d].at[h, 0], k_all, k_place[d]),
                    (kv_refs[d].at[h, 1], v_all, k_place[d]),
                )
            ):
                copy = pltpu.make_async_copy(
                    source, target.at[h, :, place], sems.at[(h * RING + d) * 3 + n]
                )
                copy.start()
                copies.append(copy)
    for copy in copies:
        copy.wait()
    for h in range(count):
        for i in range(TILES):
            rows = slice(i * TILE, (i + 1) * TILE)
            v_turned[h, :, rows] = rows_of(v_all, h, i).T

    chains = [(t, h) for t in range(together) for h in range(count)]

    def trips_of(first):
        seen = [table_ref[limits + first * together + t] for t in range(together)]
        return jnp.maximum((functools.reduce(jnp.maximum, seen) + STEP - 1) // STEP, 1)

    def fill(first, g):
        for c, (t, h) in enumerate(chains):
            pick = first * together + t
            at = pick * TILES + g * STEP
            rows = [rows_of(k_all, h, table_ref[at + u]) for u in range(STEP)]
            score_ref[c] = lax.dot_general(
                jnp.concatenate(rows, axis=0),
                rows_of(q_all, h, pick),
                (((1,), (1,)), ((), ())),
                preferred_element_type=jnp.float32,
            )

    def tiles(first, unused):
        picks = [first * together + t for t in range(together)]
        seen = [table_ref[limits + i] for i in picks]
        trips = trips_of(first)
        starts = [pl.multiple_of(i * TILE, TILE) for i in picks]

        def place(t, g, u):
            return table_ref[picks[t] * TILES + g * STEP + u]

        def step(g, carry):
            parts = [range(at, at + SUB) for at in range(0, STEP, SUB)]
            scores = [score_ref[c] for c in range(len(chains))]
            last = (g + 1 >= trips).astype(jnp.int32)
            fill(jnp.minimum(first + last, TILES // together - 1), (1 - last) * (g + 1))
            result = list(carry)
            for part in parts:
                for c, (t, h) in enumerate(chains):
                    top, total, acc = result[c]
                    score = scores[c][part[0] * TILE : (part[-1] + 1) * TILE]
                    blocks = []
                    for n, u in enumerate(part):
                        block = score[n * TILE : (n + 1) * TILE]
                        blocks.append(jnp.where(g * STEP + u < seen[t], block, -1e30))
                    largest = functools.reduce(jnp.maximum, blocks)
                    new_top = jnp.maximum(top, jnp.max(largest, axis=0, keepdims=True))
                    shrink = jnp.exp2((top - new_top) * factor)
                    weights = [jnp.exp2((block - new_top) * factor) for block in blocks]
                    added = functools.reduce(jnp.add, weights).reshape(TILE // 8, 8, TILE)
                    total = total * shrink + jnp.sum(added, axis=0)
                    weight = jnp.concatenate([w.astype(jnp.bfloat16) for w in weights], axis=0)
                    ats = [pl.multiple_of(place(t, g, u) * TILE, TILE) for u in part]
                    columns = [v_turned[h, :, pl.ds(at, TILE)] for at in ats]
                    acc = acc * shrink + jnp.dot(
                        jnp.concatenate(columns, axis=1),
                        weight,
                        preferred_element_type=jnp.float32,
                    )
                    result[c] = (new_top, total, acc)
            return result

        empty = (
            jnp.full((1, TILE), -1e30, jnp.float32),
            jnp.zeros((8, TILE), jnp.float32),
            jnp.zeros((HEAD_DIM, TILE), jnp.float32),
        )
        final = lax.fori_loop(0, trips, step, [empty] * len(chains))
        for (t, h), (top, total, acc) in zip(chains, final):
            total = jnp.sum(total, axis=0, keepdims=True)
            total = jnp.where(total > 0.0, total, 1.0)
            o_all[h, pl.ds(starts[t], TILE), :] = (acc * (1.0 / total)).T.astype(jnp.bfloat16)
            lse_ref[h, picks[t] % 2, pl.ds(picks[t] // 2, 1), :] = top * factor + jnp.log2(total)
        return unused

    fill(0, 0)
    lax.fori_loop(0, TILES // together, tiles, 0)
    for h in range(count):
        for d in range(RING):
            base = h * (SET + META)
            for j in range(GROUP):
                at = pl.multiple_of(j * RING * ROWS + q_place[d] * ROWS, ROWS)
                out_refs[d][base + j * ROWS : base + (j + 1) * ROWS, :] = o_all[
                    h, pl.ds(at, ROWS), :
                ]
            value = lse_ref[h, q_place[d] // 2]
            high = value.astype(jnp.bfloat16).astype(jnp.float32)
            middle = (value - high).astype(jnp.bfloat16).astype(jnp.float32)
            low = value - high - middle
            out_refs[d][base + SET : base + SET + META, :] = jnp.concatenate(
                [high, middle, low, jnp.zeros_like(low)], axis=0
            ).astype(jnp.bfloat16)


def attend(count, table, q, kv):
    q = [piece.reshape(count, GROUP, ROWS, HEAD_DIM) for piece in q]
    kv = [piece.reshape(count, 2, GROUP, ROWS, HEAD_DIM) for piece in kv]
    pieces = pltpu.VMEM((count, GROUP, RING, ROWS, HEAD_DIM), jnp.bfloat16)
    return call(
        functools.partial(attend_kernel, count),
        [shape(count * (SET + META), HEAD_DIM)] * RING,
        [SMEM] + [pl.BlockSpec(memory_space=pl.ANY)] * (2 * RING),
        [pieces] * 3
        + [
            pltpu.VMEM((count, RING * SET, HEAD_DIM), jnp.bfloat16),
            pltpu.VMEM((count, HEAD_DIM, RING * SET), jnp.bfloat16),
            pltpu.VMEM((count * together_in(count), STEP * TILE, TILE), jnp.float32),
            pltpu.VMEM((count, 2, GROUP, HEAD_DIM), jnp.float32),
            pltpu.SemaphoreType.DMA((count * RING * 3,)),
        ],
    )(table, *q, *kv)


def combine_kernel(table_ref, *refs):
    out_refs = refs[-GROUP:]
    shift = table_ref[TILES * TILES + TILES] % 2 * ROWS
    lanes = lax.broadcasted_iota(jnp.int32, (ROWS, HEAD_DIM), 1)
    eye = lanes == lax.broadcasted_iota(jnp.int32, (ROWS, HEAD_DIM), 0) + shift
    for p, part in enumerate(PARTS):
        pieces = refs[p * RING : (p + 1) * RING]
        for i, h in enumerate(part):
            base = i * (SET + META)
            lse = []
            for ref in pieces:
                coded = ref[base + SET : base + SET + META, :].astype(jnp.float32)
                lse.append(coded[0:8] + coded[8:16] + coded[16:24])
            top = functools.reduce(jnp.maximum, lse)
            shares = [jnp.exp2(value - top) for value in lse]
            total = functools.reduce(jnp.add, shares)
            shares = [value / total for value in shares]
            for j in range(GROUP):
                mixed = jnp.zeros((ROWS, HEAD_DIM), jnp.float32)
                for ref, share in zip(pieces, shares):
                    column = jnp.sum(jnp.where(eye, share[j : j + 1], 0.0), axis=1, keepdims=True)
                    rows = ref[base + j * ROWS : base + (j + 1) * ROWS, :]
                    mixed = mixed + column * rows.astype(jnp.float32)
                out_refs[j][:, h * HEAD_DIM : (h + 1) * HEAD_DIM] = mixed.astype(jnp.bfloat16)


def finish_kernel(at_ref, level_ref, gates_ref, *refs):
    out_ref = refs[-1]
    for j in range(GROUP):
        columns = pl.ds(pl.multiple_of(at_ref[j] * WIDTH, HEAD_DIM), WIDTH)
        gate = gates_ref[pl.ds(level_ref[0], 1), columns]
        out_ref[:, columns] = (refs[j][...].astype(jnp.float32) * gate).astype(jnp.bfloat16)


def see_table(q_slots, k_slots, retiring, mask, places):
    names = jnp.arange(TILES, dtype=jnp.int32)
    q_order = (q_slots - retiring[0]) % SPANS
    k_order = (k_slots - retiring[0]) % SPANS
    slots = jnp.arange(SPANS, dtype=jnp.int32)
    picked = (k_slots[:, None] == slots[None, :]).astype(jnp.float32)
    masked = jnp.sum(mask[:, None, :SPANS] * picked[None], axis=-1) > 0.5
    older = k_order[None, :] < q_order[:, None]
    same = k_slots[None, :] == q_slots[:, None]
    sees = same | masked & older
    before = names[None, :] < names[:, None]
    rank = jnp.sum((sees[:, None, :] & before[None]).astype(jnp.int32), axis=-1)
    chosen = sees[:, None, :] & (rank[:, None, :] == names[None, :, None])
    listed = jnp.sum(jnp.where(chosen, names[None, None, :], 0), axis=-1)
    counts = jnp.sum(sees.astype(jnp.int32), axis=-1)
    return jnp.concatenate([listed.reshape(-1), counts, places])


def local(queries, keys, values, levels, retiring, block_mask, gates):
    span = lax.axis_index("span").astype(jnp.int32)
    token = lax.axis_index("tok").astype(jnp.int32)
    y, half, core = span // 4, span // 2 % 2, span % 2
    x, z = half * 2 + token // RING, token % RING
    hop = jnp.arange(GROUP, dtype=jnp.int32)
    target = (y + hop // 2) % 4 * 2 + (core ^ hop % 2)
    hops = [dict(dy=j // 2, core=j % 2) for j in range(GROUP)]
    backs = [dict(dy=-(j // 2), core=j % 2) for j in range(GROUP)]

    meta = jnp.pad(block_mask.astype(jnp.bfloat16), ((0, 15), (0, WIDTH - SPANS)))
    packed = call(
        pack_kernel,
        [shape(3 * ROWS + 16, WIDTH)] * GROUP,
        [SMEM, VMEM, VMEM, VMEM, VMEM],
    )(target, queries[0], keys[0], values[0], meta)
    shared = [packed[0]] + [moved(packed[j], **hops[j]) for j in range(1, GROUP)]

    shapes = []
    for part in PARTS:
        shapes += [shape(len(part) * SET, HEAD_DIM), shape(len(part) * 2 * SET, HEAD_DIM)]
    spread = call(
        spread_kernel, shapes + [shape(GROUP, HEAD_DIM, jnp.float32)], [VMEM] * GROUP
    )(*shared)

    tile = jnp.arange(TILES, dtype=jnp.int32)
    base = (y - tile // 4) % 4 * 4 + (core ^ tile // 2 % 2)
    wide_slots, near_slots = base + 2 * (tile % 2), base + 2 * half
    near_mask = jnp.repeat(spread[-1], 2, axis=0)
    far_mask = jnp.repeat(moved(spread[-1], dx=2), 2, axis=0)
    wide_mask = jnp.where((tile % 2 == half)[:, None], near_mask, far_mask)
    first = core == 0
    ring = jnp.arange(RING, dtype=jnp.int32)
    table = see_table(
        jnp.where(first, wide_slots, near_slots),
        jnp.where(first, near_slots, wide_slots),
        retiring,
        jnp.where(first, wide_mask, near_mask),
        jnp.concatenate(
            [(jnp.where(first, x, z) - ring) % RING, (jnp.where(first, z, x) - ring) % RING]
        ),
    )

    pieces = []
    for p, part in enumerate(PARTS):
        own_q, own_kv = spread[2 * p], spread[2 * p + 1]
        if p > 0:
            own_q, own_kv, table = lax.optimization_barrier((own_q, own_kv, table))
        q, kv = [own_q], [own_kv]
        for d in range(1, RING):
            kv.append(moved(own_kv, dz=d, swap=1))
        for d in range(1, RING):
            q.append(moved(own_q, dx=d, swap=1))
        parts = attend(len(part), table, q, kv)
        pieces.append(parts[0])
        for d in range(1, RING):
            pieces.append(moved(parts[d], dx=-d, swap=1))

    mixed = call(
        combine_kernel, [shape(ROWS, WIDTH)] * GROUP, [SMEM] + [VMEM] * len(pieces)
    )(table, *pieces)
    returned = [mixed[0]] + [moved(mixed[j], **backs[j]) for j in range(1, GROUP)]
    result = call(finish_kernel, shape(ROWS, GROUP * WIDTH), [SMEM, SMEM] + [VMEM] * (GROUP + 1))(
        target, levels, gates, *returned
    )
    return result[None]


def solution(mesh):
    return jax.shard_map(
        local,
        mesh=mesh,
        in_specs=(
            P("span", "tok", None),
            P("span", "tok", None),
            P("span", "tok", None),
            P("span"),
            P(),
            P("span", None),
            P(),
        ),
        out_specs=P("span", "tok", None),
        check_vma=False,
    )
```

```python
import functools

import jax
import jax.numpy as jnp
from jax import lax
from jax.experimental import pallas as pl
from jax.experimental.pallas import tpu as pltpu
from jax.sharding import PartitionSpec as P


HEAD_DIM = 128
SPANS = 16
ROWS = 64
GROUP = 8
HEADS_DEV = 3
WIDTH = HEADS_DEV * HEAD_DIM
RING = 4
SET = GROUP * ROWS
META = 32
PARTS = ((0, 1), (2,))
TILE = 2 * ROWS
TILES = 16
STEP = 4
SUB = 2
LOG2E = 1.4426950408889634


BOTH = ("span", "tok")
VMEM = pl.BlockSpec(memory_space=pltpu.VMEM)
SMEM = pl.BlockSpec(memory_space=pltpu.SMEM)


def device_at(x, y, z, core):
    return (y * 4 + (x // 2) * 2 + core) * 8 + (x % 2) * 4 + z


def moved(array, dx=0, dy=0, dz=0, core=0, swap=0):
    pairs = []
    for x in range(4):
        for y in range(4):
            for z in range(4):
                for c in range(2):
                    mx, mz = (dz, dx) if swap and c else (dx, dz)
                    there = device_at((x + mx) % 4, (y + dy) % 4, (z + mz) % 4, c ^ core)
                    pairs.append((device_at(x, y, z, c), there))
    return lax.ppermute(array, BOTH, pairs)


def call(kernel, shapes, specs, scratch=()):
    return pl.pallas_call(
        kernel,
        out_shape=shapes,
        in_specs=specs,
        out_specs=jax.tree.map(lambda unused: VMEM, shapes),
        scratch_shapes=scratch,
    )


def shape(rows, columns, dtype=jnp.bfloat16):
    return jax.ShapeDtypeStruct((rows, columns), dtype)


def pack_kernel(at_ref, q_ref, k_ref, v_ref, meta_ref, *out_refs):
    for j in range(GROUP):
        columns = pl.ds(pl.multiple_of(at_ref[j] * WIDTH, HEAD_DIM), WIDTH)
        for i, ref in enumerate((q_ref, k_ref, v_ref)):
            out_refs[j][i * ROWS : (i + 1) * ROWS, :] = ref[:, columns]
        out_refs[j][3 * ROWS :, :] = meta_ref[...]


def spread_kernel(*refs):
    in_refs, out_refs = refs[:GROUP], refs[GROUP:]
    for j in range(GROUP):
        ref = in_refs[j]
        for p, part in enumerate(PARTS):
            q_ref, kv_ref = out_refs[2 * p], out_refs[2 * p + 1]
            for i, h in enumerate(part):
                columns = slice(h * HEAD_DIM, (h + 1) * HEAD_DIM)
                q_ref[i * SET + j * ROWS : i * SET + (j + 1) * ROWS, :] = ref[0:ROWS, columns]
                for t in range(2):
                    base = (2 * i + t) * SET + j * ROWS
                    kv_ref[base : base + ROWS, :] = ref[(t + 1) * ROWS : (t + 2) * ROWS, columns]
        row = ref[3 * ROWS : 3 * ROWS + 16, 0:HEAD_DIM].astype(jnp.float32)
        out_refs[-1][j : j + 1, :] = row[0:1]


def together_in(count):
    return 2 if count == 1 else 1


def attend_kernel(count, table_ref, *refs):
    together = together_in(count)
    q_refs, kv_refs = refs[:RING], refs[RING : 2 * RING]
    out_refs = refs[2 * RING : 3 * RING]
    q_all, k_all, v_all, o_all, v_turned, score_ref, lse_ref, sems = refs[3 * RING :]
    factor = jnp.float32(HEAD_DIM ** (-0.5) * LOG2E)

    def rows_of(ref, h, i):
        return ref[h, i // 2, pl.ds(i % 2 * 2, 2)].reshape(TILE, HEAD_DIM)

    limits = TILES * TILES
    q_place = [table_ref[limits + TILES + d] for d in range(RING)]
    k_place = [table_ref[limits + TILES + RING + d] for d in range(RING)]
    copies = []
    for h in range(count):
        for d in range(RING):
            for n, (source, target, place) in enumerate(
                (
                    (q_refs[d].at[h], q_all, q_place[d]),
                    (kv_refs[d].at[h, 0], k_all, k_place[d]),
                    (kv_refs[d].at[h, 1], v_all, k_place[d]),
                )
            ):
                copy = pltpu.make_async_copy(
                    source, target.at[h, :, place], sems.at[(h * RING + d) * 3 + n]
                )
                copy.start()
                copies.append(copy)
    for copy in copies:
        copy.wait()
    for h in range(count):
        for i in range(TILES):
            rows = slice(i * TILE, (i + 1) * TILE)
            v_turned[h, :, rows] = rows_of(v_all, h, i).T

    chains = [(t, h) for t in range(together) for h in range(count)]

    def trips_of(first):
        seen = [table_ref[limits + first * together + t] for t in range(together)]
        return jnp.maximum((functools.reduce(jnp.maximum, seen) + STEP - 1) // STEP, 1)

    def fill(first, g):
        for c, (t, h) in enumerate(chains):
            pick = first * together + t
            at = pick * TILES + g * STEP
            rows = [rows_of(k_all, h, table_ref[at + u]) for u in range(STEP)]
            score_ref[c] = lax.dot_general(
                jnp.concatenate(rows, axis=0),
                rows_of(q_all, h, pick),
                (((1,), (1,)), ((), ())),
                preferred_element_type=jnp.float32,
            )

    def tiles(first, unused):
        picks = [first * together + t for t in range(together)]
        seen = [table_ref[limits + i] for i in picks]
        trips = trips_of(first)
        starts = [pl.multiple_of(i * TILE, TILE) for i in picks]

        def place(t, g, u):
            return table_ref[picks[t] * TILES + g * STEP + u]

        def step(g, carry):
            parts = [range(at, at + SUB) for at in range(0, STEP, SUB)]
            scores = [score_ref[c] for c in range(len(chains))]
            last = (g + 1 >= trips).astype(jnp.int32)
            fill(jnp.minimum(first + last, TILES // together - 1), (1 - last) * (g + 1))
            result = list(carry)
            for part in parts:
                for c, (t, h) in enumerate(chains):
                    top, total, acc = result[c]
                    score = scores[c][part[0] * TILE : (part[-1] + 1) * TILE]
                    blocks = []
                    for n, u in enumerate(part):
                        block = score[n * TILE : (n + 1) * TILE]
                        blocks.append(jnp.where(g * STEP + u < seen[t], block, -1e30))
                    largest = functools.reduce(jnp.maximum, blocks)
                    new_top = jnp.maximum(top, jnp.max(largest, axis=0, keepdims=True))
                    shrink = jnp.exp2((top - new_top) * factor)
                    weights = [jnp.exp2((block - new_top) * factor) for block in blocks]
                    added = functools.reduce(jnp.add, weights).reshape(TILE // 8, 8, TILE)
                    total = total * shrink + jnp.sum(added, axis=0)
                    weight = jnp.concatenate([w.astype(jnp.bfloat16) for w in weights], axis=0)
                    ats = [pl.multiple_of(place(t, g, u) * TILE, TILE) for u in part]
                    columns = [v_turned[h, :, pl.ds(at, TILE)] for at in ats]
                    acc = acc * shrink + jnp.dot(
                        jnp.concatenate(columns, axis=1),
                        weight,
                        preferred_element_type=jnp.float32,
                    )
                    result[c] = (new_top, total, acc)
            return result

        empty = (
            jnp.full((1, TILE), -1e30, jnp.float32),
            jnp.zeros((8, TILE), jnp.float32),
            jnp.zeros((HEAD_DIM, TILE), jnp.float32),
        )
        final = lax.fori_loop(0, trips, step, [empty] * len(chains))
        for (t, h), (top, total, acc) in zip(chains, final):
            total = jnp.sum(total, axis=0, keepdims=True)
            total = jnp.where(total > 0.0, total, 1.0)
            o_all[h, pl.ds(starts[t], TILE), :] = (acc * (1.0 / total)).T.astype(jnp.bfloat16)
            lse_ref[h, picks[t] % 2, pl.ds(picks[t] // 2, 1), :] = top * factor + jnp.log2(total)
        return unused

    fill(0, 0)
    lax.fori_loop(0, TILES // together, tiles, 0)
    for h in range(count):
        for d in range(RING):
            base = h * (SET + META)
            for j in range(GROUP):
                at = pl.multiple_of(j * RING * ROWS + q_place[d] * ROWS, ROWS)
                out_refs[d][base + j * ROWS : base + (j + 1) * ROWS, :] = o_all[
                    h, pl.ds(at, ROWS), :
                ]
            value = lse_ref[h, q_place[d] // 2]
            high = value.astype(jnp.bfloat16).astype(jnp.float32)
            middle = (value - high).astype(jnp.bfloat16).astype(jnp.float32)
            low = value - high - middle
            out_refs[d][base + SET : base + SET + META, :] = jnp.concatenate(
                [high, middle, low, jnp.zeros_like(low)], axis=0
            ).astype(jnp.bfloat16)


def attend(count, table, q, kv):
    q = [piece.reshape(count, GROUP, ROWS, HEAD_DIM) for piece in q]
    kv = [piece.reshape(count, 2, GROUP, ROWS, HEAD_DIM) for piece in kv]
    pieces = pltpu.VMEM((count, GROUP, RING, ROWS, HEAD_DIM), jnp.bfloat16)
    return call(
        functools.partial(attend_kernel, count),
        [shape(count * (SET + META), HEAD_DIM)] * RING,
        [SMEM] + [pl.BlockSpec(memory_space=pl.ANY)] * (2 * RING),
        [pieces] * 3
        + [
            pltpu.VMEM((count, RING * SET, HEAD_DIM), jnp.bfloat16),
            pltpu.VMEM((count, HEAD_DIM, RING * SET), jnp.bfloat16),
            pltpu.VMEM((count * together_in(count), STEP * TILE, TILE), jnp.float32),
            pltpu.VMEM((count, 2, GROUP, HEAD_DIM), jnp.float32),
            pltpu.SemaphoreType.DMA((count * RING * 3,)),
        ],
    )(table, *q, *kv)


def combine_kernel(table_ref, *refs):
    out_refs = refs[-GROUP:]
    shift = table_ref[TILES * TILES + TILES] % 2 * ROWS
    lanes = lax.broadcasted_iota(jnp.int32, (ROWS, HEAD_DIM), 1)
    eye = lanes == lax.broadcasted_iota(jnp.int32, (ROWS, HEAD_DIM), 0) + shift
    for p, part in enumerate(PARTS):
        pieces = refs[p * RING : (p + 1) * RING]
        for i, h in enumerate(part):
            base = i * (SET + META)
            lse = []
            for ref in pieces:
                coded = ref[base + SET : base + SET + META, :].astype(jnp.float32)
                lse.append(coded[0:8] + coded[8:16] + coded[16:24])
            top = functools.reduce(jnp.maximum, lse)
            shares = [jnp.exp2(value - top) for value in lse]
            total = functools.reduce(jnp.add, shares)
            shares = [value / total for value in shares]
            for j in range(GROUP):
                mixed = jnp.zeros((ROWS, HEAD_DIM), jnp.float32)
                for ref, share in zip(pieces, shares):
                    column = jnp.sum(jnp.where(eye, share[j : j + 1], 0.0), axis=1, keepdims=True)
                    rows = ref[base + j * ROWS : base + (j + 1) * ROWS, :]
                    mixed = mixed + column * rows.astype(jnp.float32)
                out_refs[j][:, h * HEAD_DIM : (h + 1) * HEAD_DIM] = mixed.astype(jnp.bfloat16)


def finish_kernel(at_ref, level_ref, gates_ref, *refs):
    out_ref = refs[-1]
    for j in range(GROUP):
        columns = pl.ds(pl.multiple_of(at_ref[j] * WIDTH, HEAD_DIM), WIDTH)
        gate = gates_ref[pl.ds(level_ref[0], 1), columns]
        out_ref[:, columns] = (refs[j][...].astype(jnp.float32) * gate).astype(jnp.bfloat16)


def see_table(q_slots, k_slots, retiring, mask, places):
    names = jnp.arange(TILES, dtype=jnp.int32)
    q_order = (q_slots - retiring[0]) % SPANS
    k_order = (k_slots - retiring[0]) % SPANS
    slots = jnp.arange(SPANS, dtype=jnp.int32)
    picked = (k_slots[:, None] == slots[None, :]).astype(jnp.float32)
    masked = jnp.sum(mask[:, None, :SPANS] * picked[None], axis=-1) > 0.5
    older = k_order[None, :] < q_order[:, None]
    same = k_slots[None, :] == q_slots[:, None]
    sees = same | masked & older
    before = names[None, :] < names[:, None]
    rank = jnp.sum((sees[:, None, :] & before[None]).astype(jnp.int32), axis=-1)
    chosen = sees[:, None, :] & (rank[:, None, :] == names[None, :, None])
    listed = jnp.sum(jnp.where(chosen, names[None, None, :], 0), axis=-1)
    counts = jnp.sum(sees.astype(jnp.int32), axis=-1)
    return jnp.concatenate([listed.reshape(-1), counts, places])


def local(queries, keys, values, levels, retiring, block_mask, gates):
    span = lax.axis_index("span").astype(jnp.int32)
    token = lax.axis_index("tok").astype(jnp.int32)
    y, half, core = span // 4, span // 2 % 2, span % 2
    x, z = half * 2 + token // RING, token % RING
    hop = jnp.arange(GROUP, dtype=jnp.int32)
    target = (y + hop // 2) % 4 * 2 + (core ^ hop % 2)
    hops = [dict(dy=j // 2, core=j % 2) for j in range(GROUP)]
    backs = [dict(dy=-(j // 2), core=j % 2) for j in range(GROUP)]

    meta = jnp.pad(block_mask.astype(jnp.bfloat16), ((0, 15), (0, WIDTH - SPANS)))
    packed = call(
        pack_kernel,
        [shape(3 * ROWS + 16, WIDTH)] * GROUP,
        [SMEM, VMEM, VMEM, VMEM, VMEM],
    )(target, queries[0], keys[0], values[0], meta)
    shared = [packed[0]]
    for j in range(1, GROUP):
        shared.append(moved(packed[j], **hops[j]))

    shapes = []
    for part in PARTS:
        shapes += [shape(len(part) * SET, HEAD_DIM), shape(len(part) * 2 * SET, HEAD_DIM)]
    spread = call(
        spread_kernel, shapes + [shape(GROUP, HEAD_DIM, jnp.float32)], [VMEM] * GROUP
    )(*shared)

    tile = jnp.arange(TILES, dtype=jnp.int32)
    base = (y - tile // 4) % 4 * 4 + (core ^ tile // 2 % 2)
    wide_slots, near_slots = base + 2 * (tile % 2), base + 2 * half
    near_mask = jnp.repeat(spread[-1], 2, axis=0)
    far_mask = jnp.repeat(moved(spread[-1], dx=2), 2, axis=0)
    wide_mask = jnp.where((tile % 2 == half)[:, None], near_mask, far_mask)
    first = core == 0
    ring = jnp.arange(RING, dtype=jnp.int32)
    table = see_table(
        jnp.where(first, wide_slots, near_slots),
        jnp.where(first, near_slots, wide_slots),
        retiring,
        jnp.where(first, wide_mask, near_mask),
        jnp.concatenate(
            [(jnp.where(first, x, z) - ring) % RING, (jnp.where(first, z, x) - ring) % RING]
        ),
    )

    pieces = []
    for p, part in enumerate(PARTS):
        own_q, own_kv = spread[2 * p], spread[2 * p + 1]
        if p > 0:
            own_q, own_kv, table = lax.optimization_barrier((own_q, own_kv, table))
        q, kv = [own_q], [own_kv]
        for d in range(1, RING):
            kv.append(moved(own_kv, dz=d, swap=1))
        for d in range(1, RING):
            q.append(moved(own_q, dx=d, swap=1))
        parts = attend(len(part), table, q, kv)
        pieces.append(parts[0])
        for d in range(1, RING):
            pieces.append(moved(parts[d], dx=-d, swap=1))

    mixed = call(
        combine_kernel, [shape(ROWS, WIDTH)] * GROUP, [SMEM] + [VMEM] * len(pieces)
    )(table, *pieces)
    returned = [mixed[0]]
    for j in range(1, GROUP):
        returned.append(moved(mixed[j], **backs[j]))
    result = call(finish_kernel, shape(ROWS, GROUP * WIDTH), [SMEM, SMEM] + [VMEM] * (GROUP + 1))(
        target, levels, gates, *returned
    )
    return result[None]


def solution(mesh):
    return jax.shard_map(
        local,
        mesh=mesh,
        in_specs=(
            P("span", "tok", None),
            P("span", "tok", None),
            P("span", "tok", None),
            P("span"),
            P(),
            P("span", None),
            P(),
        ),
        out_specs=P("span", "tok", None),
        check_vma=False,
    )
```

```python
import functools

import jax
import jax.numpy as jnp
from jax import lax
from jax.experimental import pallas as pl
from jax.experimental.pallas import tpu as pltpu
from jax.sharding import PartitionSpec as P


HEAD_DIM = 128
SPANS = 16
ROWS = 64
GROUP = 8
HEADS_DEV = 3
WIDTH = HEADS_DEV * HEAD_DIM
RING = 4
SET = GROUP * ROWS
META = 32
PARTS = ((0, 1, 2),)
TILE = 2 * ROWS
TILES = 16
STEP = 4
SUB = 2
LOG2E = 1.4426950408889634


BOTH = ("span", "tok")
VMEM = pl.BlockSpec(memory_space=pltpu.VMEM)
SMEM = pl.BlockSpec(memory_space=pltpu.SMEM)


def device_at(x, y, z, core):
    return (y * 4 + (x // 2) * 2 + core) * 8 + (x % 2) * 4 + z


def moved(array, dx=0, dy=0, dz=0, core=0, swap=0):
    pairs = []
    for x in range(4):
        for y in range(4):
            for z in range(4):
                for c in range(2):
                    mx, mz = (dz, dx) if swap and c else (dx, dz)
                    there = device_at((x + mx) % 4, (y + dy) % 4, (z + mz) % 4, c ^ core)
                    pairs.append((device_at(x, y, z, c), there))
    return lax.ppermute(array, BOTH, pairs)


def call(kernel, shapes, specs, scratch=()):
    return pl.pallas_call(
        kernel,
        out_shape=shapes,
        in_specs=specs,
        out_specs=jax.tree.map(lambda unused: VMEM, shapes),
        scratch_shapes=scratch,
    )


def shape(rows, columns, dtype=jnp.bfloat16):
    return jax.ShapeDtypeStruct((rows, columns), dtype)


def pack_kernel(at_ref, mask_ref, q_ref, k_ref, v_ref, *out_refs):
    lanes = lax.broadcasted_iota(jnp.int32, (16, WIDTH), 1)
    meta = jnp.zeros((16, WIDTH), jnp.int32)
    for t in range(SPANS):
        meta = jnp.where(lanes == t, mask_ref[0, t], meta)
    meta = meta.astype(jnp.float32).astype(jnp.bfloat16)
    for j in range(GROUP):
        columns = pl.ds(pl.multiple_of(at_ref[j] * WIDTH, HEAD_DIM), WIDTH)
        for i, ref in enumerate((q_ref, k_ref, v_ref)):
            out_refs[j][i * ROWS : (i + 1) * ROWS, :] = ref[:, columns]
        out_refs[j][3 * ROWS :, :] = meta


def spread_kernel(*refs):
    in_refs, out_refs = refs[:GROUP], refs[GROUP:]
    for j in range(GROUP):
        ref = in_refs[j]
        for p, part in enumerate(PARTS):
            q_ref, kv_ref = out_refs[2 * p], out_refs[2 * p + 1]
            for i, h in enumerate(part):
                columns = slice(h * HEAD_DIM, (h + 1) * HEAD_DIM)
                q_ref[i * SET + j * ROWS : i * SET + (j + 1) * ROWS, :] = ref[0:ROWS, columns]
                for t in range(2):
                    base = (2 * i + t) * SET + j * ROWS
                    kv_ref[base : base + ROWS, :] = ref[(t + 1) * ROWS : (t + 2) * ROWS, columns]
        row = ref[3 * ROWS : 3 * ROWS + 16, 0:HEAD_DIM].astype(jnp.float32)
        out_refs[-1][j : j + 1, :] = row[0:1]


def together_in(count):
    return 2 if count == 1 else 1


def attend_kernel(count, table_ref, *refs):
    together = together_in(count)
    q_refs, kv_refs = refs[:RING], refs[RING : 2 * RING]
    out_refs = refs[2 * RING : 3 * RING]
    q_all, k_all, v_all, o_all, v_turned, score_ref, lse_ref, sems = refs[3 * RING :]
    factor = jnp.float32(HEAD_DIM ** (-0.5) * LOG2E)

    def rows_of(ref, h, i):
        return ref[h, i // 2, pl.ds(i % 2 * 2, 2)].reshape(TILE, HEAD_DIM)

    limits = TILES * TILES
    q_place = [table_ref[limits + TILES + d] for d in range(RING)]
    k_place = [table_ref[limits + TILES + RING + d] for d in range(RING)]
    copies = []
    for h in range(count):
        for d in range(RING):
            for n, (source, target, place) in enumerate(
                (
                    (q_refs[d].at[h], q_all, q_place[d]),
                    (kv_refs[d].at[h, 0], k_all, k_place[d]),
                    (kv_refs[d].at[h, 1], v_all, k_place[d]),
                )
            ):
                copy = pltpu.make_async_copy(
                    source, target.at[h, :, place], sems.at[(h * RING + d) * 3 + n]
                )
                copy.start()
                copies.append(copy)
    for copy in copies:
        copy.wait()
    for h in range(count):
        for i in range(TILES):
            rows = slice(i * TILE, (i + 1) * TILE)
            v_turned[h, :, rows] = rows_of(v_all, h, i).T

    chains = [(t, h) for t in range(together) for h in range(count)]

    def trips_of(first):
        seen = [table_ref[limits + first * together + t] for t in range(together)]
        return jnp.maximum((functools.reduce(jnp.maximum, seen) + STEP - 1) // STEP, 1)

    def fill(first, g):
        for c, (t, h) in enumerate(chains):
            pick = first * together + t
            at = pick * TILES + g * STEP
            rows = [rows_of(k_all, h, table_ref[at + u]) for u in range(STEP)]
            score_ref[c] = lax.dot_general(
                jnp.concatenate(rows, axis=0),
                rows_of(q_all, h, pick),
                (((1,), (1,)), ((), ())),
                preferred_element_type=jnp.float32,
            )

    def tiles(first, unused):
        picks = [first * together + t for t in range(together)]
        seen = [table_ref[limits + i] for i in picks]
        trips = trips_of(first)
        starts = [pl.multiple_of(i * TILE, TILE) for i in picks]

        def place(t, g, u):
            return table_ref[picks[t] * TILES + g * STEP + u]

        def step(g, carry):
            parts = [range(at, at + SUB) for at in range(0, STEP, SUB)]
            scores = [score_ref[c] for c in range(len(chains))]
            last = (g + 1 >= trips).astype(jnp.int32)
            fill(jnp.minimum(first + last, TILES // together - 1), (1 - last) * (g + 1))
            result = list(carry)
            for part in parts:
                for c, (t, h) in enumerate(chains):
                    top, total, acc = result[c]
                    score = scores[c][part[0] * TILE : (part[-1] + 1) * TILE]
                    blocks = []
                    for n, u in enumerate(part):
                        block = score[n * TILE : (n + 1) * TILE]
                        blocks.append(jnp.where(g * STEP + u < seen[t], block, -1e30))
                    largest = functools.reduce(jnp.maximum, blocks)
                    new_top = jnp.maximum(top, jnp.max(largest, axis=0, keepdims=True))
                    shrink = jnp.exp2((top - new_top) * factor)
                    weights = [jnp.exp2((block - new_top) * factor) for block in blocks]
                    added = functools.reduce(jnp.add, weights).reshape(TILE // 8, 8, TILE)
                    total = total * shrink + jnp.sum(added, axis=0)
                    weight = jnp.concatenate([w.astype(jnp.bfloat16) for w in weights], axis=0)
                    ats = [pl.multiple_of(place(t, g, u) * TILE, TILE) for u in part]
                    columns = [v_turned[h, :, pl.ds(at, TILE)] for at in ats]
                    acc = acc * shrink + jnp.dot(
                        jnp.concatenate(columns, axis=1),
                        weight,
                        preferred_element_type=jnp.float32,
                    )
                    result[c] = (new_top, total, acc)
            return result

        empty = (
            jnp.full((1, TILE), -1e30, jnp.float32),
            jnp.zeros((8, TILE), jnp.float32),
            jnp.zeros((HEAD_DIM, TILE), jnp.float32),
        )
        final = lax.fori_loop(0, trips, step, [empty] * len(chains))
        for (t, h), (top, total, acc) in zip(chains, final):
            total = jnp.sum(total, axis=0, keepdims=True)
            total = jnp.where(total > 0.0, total, 1.0)
            o_all[h, pl.ds(starts[t], TILE), :] = (acc * (1.0 / total)).T.astype(jnp.bfloat16)
            lse_ref[h, picks[t] % 2, pl.ds(picks[t] // 2, 1), :] = top * factor + jnp.log2(total)
        return unused

    fill(0, 0)
    lax.fori_loop(0, TILES // together, tiles, 0)
    for h in range(count):
        for d in range(RING):
            base = h * (SET + META)
            for j in range(GROUP):
                at = pl.multiple_of(j * RING * ROWS + q_place[d] * ROWS, ROWS)
                out_refs[d][base + j * ROWS : base + (j + 1) * ROWS, :] = o_all[
                    h, pl.ds(at, ROWS), :
                ]
            value = lse_ref[h, q_place[d] // 2]
            high = value.astype(jnp.bfloat16).astype(jnp.float32)
            middle = (value - high).astype(jnp.bfloat16).astype(jnp.float32)
            low = value - high - middle
            out_refs[d][base + SET : base + SET + META, :] = jnp.concatenate(
                [high, middle, low, jnp.zeros_like(low)], axis=0
            ).astype(jnp.bfloat16)


def attend(count, table, q, kv):
    q = [piece.reshape(count, GROUP, ROWS, HEAD_DIM) for piece in q]
    kv = [piece.reshape(count, 2, GROUP, ROWS, HEAD_DIM) for piece in kv]
    pieces = pltpu.VMEM((count, GROUP, RING, ROWS, HEAD_DIM), jnp.bfloat16)
    return call(
        functools.partial(attend_kernel, count),
        [shape(count * (SET + META), HEAD_DIM)] * RING,
        [SMEM] + [pl.BlockSpec(memory_space=pl.ANY)] * (2 * RING),
        [pieces] * 3
        + [
            pltpu.VMEM((count, RING * SET, HEAD_DIM), jnp.bfloat16),
            pltpu.VMEM((count, HEAD_DIM, RING * SET), jnp.bfloat16),
            pltpu.VMEM((count * together_in(count), STEP * TILE, TILE), jnp.float32),
            pltpu.VMEM((count, 2, GROUP, HEAD_DIM), jnp.float32),
            pltpu.SemaphoreType.DMA((count * RING * 3,)),
        ],
    )(table, *q, *kv)


def combine_kernel(table_ref, *refs):
    out_refs = refs[-GROUP:]
    shift = table_ref[TILES * TILES + TILES] % 2 * ROWS
    lanes = lax.broadcasted_iota(jnp.int32, (ROWS, HEAD_DIM), 1)
    eye = lanes == lax.broadcasted_iota(jnp.int32, (ROWS, HEAD_DIM), 0) + shift
    for p, part in enumerate(PARTS):
        pieces = refs[p * RING : (p + 1) * RING]
        for i, h in enumerate(part):
            base = i * (SET + META)
            lse = []
            for ref in pieces:
                coded = ref[base + SET : base + SET + META, :].astype(jnp.float32)
                lse.append(coded[0:8] + coded[8:16] + coded[16:24])
            top = functools.reduce(jnp.maximum, lse)
            shares = [jnp.exp2(value - top) for value in lse]
            total = functools.reduce(jnp.add, shares)
            shares = [value / total for value in shares]
            for j in range(GROUP):
                mixed = jnp.zeros((ROWS, HEAD_DIM), jnp.float32)
                for ref, share in zip(pieces, shares):
                    column = jnp.sum(jnp.where(eye, share[j : j + 1], 0.0), axis=1, keepdims=True)
                    rows = ref[base + j * ROWS : base + (j + 1) * ROWS, :]
                    mixed = mixed + column * rows.astype(jnp.float32)
                out_refs[j][:, h * HEAD_DIM : (h + 1) * HEAD_DIM] = mixed.astype(jnp.bfloat16)


def finish_kernel(at_ref, level_ref, gates_ref, *refs):
    out_ref = refs[-1]
    for j in range(GROUP):
        columns = pl.ds(pl.multiple_of(at_ref[j] * WIDTH, HEAD_DIM), WIDTH)
        gate = gates_ref[pl.ds(level_ref[0], 1), columns]
        out_ref[:, columns] = (refs[j][...].astype(jnp.float32) * gate).astype(jnp.bfloat16)


def see_table(q_slots, k_slots, retiring, mask, places):
    names = jnp.arange(TILES, dtype=jnp.int32)
    q_order = (q_slots - retiring[0]) % SPANS
    k_order = (k_slots - retiring[0]) % SPANS
    slots = jnp.arange(SPANS, dtype=jnp.int32)
    picked = (k_slots[:, None] == slots[None, :]).astype(jnp.float32)
    masked = jnp.sum(mask[:, None, :SPANS] * picked[None], axis=-1) > 0.5
    older = k_order[None, :] < q_order[:, None]
    same = k_slots[None, :] == q_slots[:, None]
    sees = same | masked & older
    before = names[None, :] < names[:, None]
    rank = jnp.sum((sees[:, None, :] & before[None]).astype(jnp.int32), axis=-1)
    chosen = sees[:, None, :] & (rank[:, None, :] == names[None, :, None])
    listed = jnp.sum(jnp.where(chosen, names[None, None, :], 0), axis=-1)
    counts = jnp.sum(sees.astype(jnp.int32), axis=-1)
    return jnp.concatenate([listed.reshape(-1), counts, places])


def local(queries, keys, values, levels, retiring, block_mask, gates):
    span = lax.axis_index("span").astype(jnp.int32)
    token = lax.axis_index("tok").astype(jnp.int32)
    y, half, core = span // 4, span // 2 % 2, span % 2
    x, z = half * 2 + token // RING, token % RING
    hop = jnp.arange(GROUP, dtype=jnp.int32)
    target = (y + hop // 2) % 4 * 2 + (core ^ hop % 2)
    hops = [dict(dy=j // 2, core=j % 2) for j in range(GROUP)]
    backs = [dict(dy=-(j // 2), core=j % 2) for j in range(GROUP)]

    packed = call(
        pack_kernel,
        [shape(3 * ROWS + 16, WIDTH)] * GROUP,
        [SMEM, SMEM, VMEM, VMEM, VMEM],
    )(target, block_mask, queries[0], keys[0], values[0])
    shared = [packed[0]]
    for j in range(1, GROUP):
        shared.append(moved(packed[j], **hops[j]))

    shapes = []
    for part in PARTS:
        shapes += [shape(len(part) * SET, HEAD_DIM), shape(len(part) * 2 * SET, HEAD_DIM)]
    spread = call(
        spread_kernel, shapes + [shape(GROUP, HEAD_DIM, jnp.float32)], [VMEM] * GROUP
    )(*shared)

    tile = jnp.arange(TILES, dtype=jnp.int32)
    base = (y - tile // 4) % 4 * 4 + (core ^ tile // 2 % 2)
    wide_slots, near_slots = base + 2 * (tile % 2), base + 2 * half
    near_mask = jnp.repeat(spread[-1], 2, axis=0)
    far_mask = jnp.repeat(moved(spread[-1], dx=2), 2, axis=0)
    wide_mask = jnp.where((tile % 2 == half)[:, None], near_mask, far_mask)
    first = core == 0
    ring = jnp.arange(RING, dtype=jnp.int32)
    table = see_table(
        jnp.where(first, wide_slots, near_slots),
        jnp.where(first, near_slots, wide_slots),
        retiring,
        jnp.where(first, wide_mask, near_mask),
        jnp.concatenate(
            [(jnp.where(first, x, z) - ring) % RING, (jnp.where(first, z, x) - ring) % RING]
        ),
    )

    pieces = []
    for p, part in enumerate(PARTS):
        own_q, own_kv = spread[2 * p], spread[2 * p + 1]
        if p > 0:
            own_q, own_kv, table = lax.optimization_barrier((own_q, own_kv, table))
        q, kv = [own_q], [own_kv]
        for d in range(1, RING):
            kv.append(moved(own_kv, dz=d, swap=1))
        for d in range(1, RING):
            q.append(moved(own_q, dx=d, swap=1))
        parts = attend(len(part), table, q, kv)
        pieces.append(parts[0])
        for d in range(1, RING):
            pieces.append(moved(parts[d], dx=-d, swap=1))

    mixed = call(
        combine_kernel, [shape(ROWS, WIDTH)] * GROUP, [SMEM] + [VMEM] * len(pieces)
    )(table, *pieces)
    returned = [mixed[0]]
    for j in range(1, GROUP):
        returned.append(moved(mixed[j], **backs[j]))
    result = call(finish_kernel, shape(ROWS, GROUP * WIDTH), [SMEM, SMEM] + [VMEM] * (GROUP + 1))(
        target, levels, gates, *returned
    )
    return result[None]


def solution(mesh):
    return jax.shard_map(
        local,
        mesh=mesh,
        in_specs=(
            P("span", "tok", None),
            P("span", "tok", None),
            P("span", "tok", None),
            P("span"),
            P(),
            P("span", None),
            P(),
        ),
        out_specs=P("span", "tok", None),
        check_vma=False,
    )
```

```python
import functools

import jax
import jax.numpy as jnp
from jax import lax
from jax.experimental import pallas as pl
from jax.experimental.pallas import tpu as pltpu
from jax.sharding import PartitionSpec as P


HEAD_DIM = 128
SPANS = 16
ROWS = 64
GROUP = 8
HEADS_DEV = 3
WIDTH = HEADS_DEV * HEAD_DIM
RING = 4
SET = GROUP * ROWS
META = 32
PARTS = ((0, 1, 2),)
TILE = 2 * ROWS
TILES = 16
STEP = 4
SUB = 2
LOG2E = 1.4426950408889634


BOTH = ("span", "tok")
VMEM = pl.BlockSpec(memory_space=pltpu.VMEM)
SMEM = pl.BlockSpec(memory_space=pltpu.SMEM)


def device_at(x, y, z, core):
    return (y * 4 + (x // 2) * 2 + core) * 8 + (x % 2) * 4 + z


def moved(array, dx=0, dy=0, dz=0, core=0, swap=0):
    pairs = []
    for x in range(4):
        for y in range(4):
            for z in range(4):
                for c in range(2):
                    mx, mz = (dz, dx) if swap and c else (dx, dz)
                    there = device_at((x + mx) % 4, (y + dy) % 4, (z + mz) % 4, c ^ core)
                    pairs.append((device_at(x, y, z, c), there))
    return lax.ppermute(array, BOTH, pairs)


def call(kernel, shapes, specs, scratch=()):
    return pl.pallas_call(
        kernel,
        out_shape=shapes,
        in_specs=specs,
        out_specs=jax.tree.map(lambda unused: VMEM, shapes),
        scratch_shapes=scratch,
    )


def shape(rows, columns, dtype=jnp.bfloat16):
    return jax.ShapeDtypeStruct((rows, columns), dtype)


def pack_kernel(at_ref, mask_ref, q_ref, k_ref, v_ref, *out_refs):
    lanes = lax.broadcasted_iota(jnp.int32, (16, WIDTH), 1)
    meta = jnp.zeros((16, WIDTH), jnp.int32)
    for t in range(SPANS):
        meta = jnp.where(lanes == t, mask_ref[0, t], meta)
    meta = meta.astype(jnp.float32).astype(jnp.bfloat16)
    for j in range(GROUP):
        columns = pl.ds(pl.multiple_of(at_ref[j] * WIDTH, HEAD_DIM), WIDTH)
        for i, ref in enumerate((q_ref, k_ref, v_ref)):
            out_refs[j][i * ROWS : (i + 1) * ROWS, :] = ref[:, columns]
        out_refs[j][3 * ROWS :, :] = meta


def spread_kernel(*refs):
    in_refs, out_refs = refs[:GROUP], refs[GROUP:]
    for j in range(GROUP):
        ref = in_refs[j]
        for p, part in enumerate(PARTS):
            q_ref, kv_ref = out_refs[2 * p], out_refs[2 * p + 1]
            for i, h in enumerate(part):
                columns = slice(h * HEAD_DIM, (h + 1) * HEAD_DIM)
                q_ref[i * SET + j * ROWS : i * SET + (j + 1) * ROWS, :] = ref[0:ROWS, columns]
                for t in range(2):
                    base = (2 * i + t) * SET + j * ROWS
                    kv_ref[base : base + ROWS, :] = ref[(t + 1) * ROWS : (t + 2) * ROWS, columns]
        row = ref[3 * ROWS : 3 * ROWS + 16, 0:HEAD_DIM].astype(jnp.float32)
        out_refs[-1][j : j + 1, :] = row[0:1]


def together_in(count):
    return 2 if count == 1 else 1


def attend_kernel(count, table_ref, *refs):
    together = together_in(count)
    q_refs, kv_refs = refs[:RING], refs[RING : 2 * RING]
    out_refs = refs[2 * RING : 3 * RING]
    q_all, k_all, v_all, o_all, v_turned, score_ref, lse_ref, sems = refs[3 * RING :]
    factor = jnp.float32(HEAD_DIM ** (-0.5) * LOG2E)

    def rows_of(ref, h, i):
        return ref[h, i // 2, pl.ds(i % 2 * 2, 2)].reshape(TILE, HEAD_DIM)

    limits = TILES * TILES
    q_place = [table_ref[limits + TILES + d] for d in range(RING)]
    k_place = [table_ref[limits + TILES + RING + d] for d in range(RING)]
    copies = []
    for n in range(3):
        for h in range(count):
            for d in range(RING):
                source, target, place = (
                    (kv_refs[d].at[h, 1], v_all, k_place[d]),
                    (kv_refs[d].at[h, 0], k_all, k_place[d]),
                    (q_refs[d].at[h], q_all, q_place[d]),
                )[n]
                copy = pltpu.make_async_copy(
                    source, target.at[h, :, place], sems.at[len(copies)]
                )
                copy.start()
                copies.append(copy)
    for copy in copies[: count * RING]:
        copy.wait()
    for h in range(count):
        for i in range(TILES):
            rows = slice(i * TILE, (i + 1) * TILE)
            v_turned[h, :, rows] = rows_of(v_all, h, i).T
    for copy in copies[count * RING :]:
        copy.wait()

    chains = [(t, h) for t in range(together) for h in range(count)]

    def trips_of(first):
        seen = [table_ref[limits + first * together + t] for t in range(together)]
        return jnp.maximum((functools.reduce(jnp.maximum, seen) + STEP - 1) // STEP, 1)

    def fill(first, g):
        for c, (t, h) in enumerate(chains):
            pick = first * together + t
            at = pick * TILES + g * STEP
            rows = [rows_of(k_all, h, table_ref[at + u]) for u in range(STEP)]
            score_ref[c] = lax.dot_general(
                jnp.concatenate(rows, axis=0),
                rows_of(q_all, h, pick),
                (((1,), (1,)), ((), ())),
                preferred_element_type=jnp.float32,
            )

    def tiles(first, unused):
        picks = [first * together + t for t in range(together)]
        seen = [table_ref[limits + i] for i in picks]
        trips = trips_of(first)
        starts = [pl.multiple_of(i * TILE, TILE) for i in picks]

        def place(t, g, u):
            return table_ref[picks[t] * TILES + g * STEP + u]

        def step(g, carry):
            parts = [range(at, at + SUB) for at in range(0, STEP, SUB)]
            scores = [score_ref[c] for c in range(len(chains))]
            last = (g + 1 >= trips).astype(jnp.int32)
            fill(jnp.minimum(first + last, TILES // together - 1), (1 - last) * (g + 1))
            result = list(carry)
            for part in parts:
                for c, (t, h) in enumerate(chains):
                    top, total, acc = result[c]
                    score = scores[c][part[0] * TILE : (part[-1] + 1) * TILE]
                    blocks = []
                    for n, u in enumerate(part):
                        block = score[n * TILE : (n + 1) * TILE]
                        blocks.append(jnp.where(g * STEP + u < seen[t], block, -1e30))
                    largest = functools.reduce(jnp.maximum, blocks)
                    new_top = jnp.maximum(top, jnp.max(largest, axis=0, keepdims=True))
                    shrink = jnp.exp2((top - new_top) * factor)
                    weights = [jnp.exp2((block - new_top) * factor) for block in blocks]
                    added = functools.reduce(jnp.add, weights).reshape(TILE // 8, 8, TILE)
                    total = total * shrink + jnp.sum(added, axis=0)
                    weight = jnp.concatenate([w.astype(jnp.bfloat16) for w in weights], axis=0)
                    ats = [pl.multiple_of(place(t, g, u) * TILE, TILE) for u in part]
                    columns = [v_turned[h, :, pl.ds(at, TILE)] for at in ats]
                    acc = acc * shrink + jnp.dot(
                        jnp.concatenate(columns, axis=1),
                        weight,
                        preferred_element_type=jnp.float32,
                    )
                    result[c] = (new_top, total, acc)
            return result

        empty = (
            jnp.full((1, TILE), -1e30, jnp.float32),
            jnp.zeros((8, TILE), jnp.float32),
            jnp.zeros((HEAD_DIM, TILE), jnp.float32),
        )
        final = lax.fori_loop(0, trips, step, [empty] * len(chains))
        for (t, h), (top, total, acc) in zip(chains, final):
            total = jnp.sum(total, axis=0, keepdims=True)
            total = jnp.where(total > 0.0, total, 1.0)
            o_all[h, pl.ds(starts[t], TILE), :] = (acc * (1.0 / total)).T.astype(jnp.bfloat16)
            lse_ref[h, picks[t] % 2, pl.ds(picks[t] // 2, 1), :] = top * factor + jnp.log2(total)
        return unused

    fill(0, 0)
    lax.fori_loop(0, TILES // together, tiles, 0)
    for h in range(count):
        for d in range(RING):
            base = h * (SET + META)
            for j in range(GROUP):
                at = pl.multiple_of(j * RING * ROWS + q_place[d] * ROWS, ROWS)
                out_refs[d][base + j * ROWS : base + (j + 1) * ROWS, :] = o_all[
                    h, pl.ds(at, ROWS), :
                ]
            value = lse_ref[h, q_place[d] // 2]
            high = value.astype(jnp.bfloat16).astype(jnp.float32)
            middle = (value - high).astype(jnp.bfloat16).astype(jnp.float32)
            low = value - high - middle
            out_refs[d][base + SET : base + SET + META, :] = jnp.concatenate(
                [high, middle, low, jnp.zeros_like(low)], axis=0
            ).astype(jnp.bfloat16)


def attend(count, table, q, kv):
    q = [piece.reshape(count, GROUP, ROWS, HEAD_DIM) for piece in q]
    kv = [piece.reshape(count, 2, GROUP, ROWS, HEAD_DIM) for piece in kv]
    pieces = pltpu.VMEM((count, GROUP, RING, ROWS, HEAD_DIM), jnp.bfloat16)
    return call(
        functools.partial(attend_kernel, count),
        [shape(count * (SET + META), HEAD_DIM)] * RING,
        [SMEM] + [pl.BlockSpec(memory_space=pl.ANY)] * (2 * RING),
        [pieces] * 3
        + [
            pltpu.VMEM((count, RING * SET, HEAD_DIM), jnp.bfloat16),
            pltpu.VMEM((count, HEAD_DIM, RING * SET), jnp.bfloat16),
            pltpu.VMEM((count * together_in(count), STEP * TILE, TILE), jnp.float32),
            pltpu.VMEM((count, 2, GROUP, HEAD_DIM), jnp.float32),
            pltpu.SemaphoreType.DMA((count * RING * 3,)),
        ],
    )(table, *q, *kv)


def combine_kernel(table_ref, *refs):
    out_refs = refs[-GROUP:]
    shift = table_ref[TILES * TILES + TILES] % 2 * ROWS
    lanes = lax.broadcasted_iota(jnp.int32, (ROWS, HEAD_DIM), 1)
    eye = lanes == lax.broadcasted_iota(jnp.int32, (ROWS, HEAD_DIM), 0) + shift
    for p, part in enumerate(PARTS):
        pieces = refs[p * RING : (p + 1) * RING]
        for i, h in enumerate(part):
            base = i * (SET + META)
            lse = []
            for ref in pieces:
                coded = ref[base + SET : base + SET + META, :].astype(jnp.float32)
                lse.append(coded[0:8] + coded[8:16] + coded[16:24])
            top = functools.reduce(jnp.maximum, lse)
            shares = [jnp.exp2(value - top) for value in lse]
            total = functools.reduce(jnp.add, shares)
            shares = [value / total for value in shares]
            for j in range(GROUP):
                mixed = jnp.zeros((ROWS, HEAD_DIM), jnp.float32)
                for ref, share in zip(pieces, shares):
                    column = jnp.sum(jnp.where(eye, share[j : j + 1], 0.0), axis=1, keepdims=True)
                    rows = ref[base + j * ROWS : base + (j + 1) * ROWS, :]
                    mixed = mixed + column * rows.astype(jnp.float32)
                out_refs[j][:, h * HEAD_DIM : (h + 1) * HEAD_DIM] = mixed.astype(jnp.bfloat16)


def finish_kernel(at_ref, level_ref, gates_ref, *refs):
    out_ref = refs[-1]
    for j in range(GROUP):
        columns = pl.ds(pl.multiple_of(at_ref[j] * WIDTH, HEAD_DIM), WIDTH)
        gate = gates_ref[pl.ds(level_ref[0], 1), columns]
        out_ref[:, columns] = (refs[j][...].astype(jnp.float32) * gate).astype(jnp.bfloat16)


def see_table(q_slots, k_slots, retiring, mask, places):
    names = jnp.arange(TILES, dtype=jnp.int32)
    q_order = (q_slots - retiring[0]) % SPANS
    k_order = (k_slots - retiring[0]) % SPANS
    slots = jnp.arange(SPANS, dtype=jnp.int32)
    picked = (k_slots[:, None] == slots[None, :]).astype(jnp.float32)
    masked = jnp.sum(mask[:, None, :SPANS] * picked[None], axis=-1) > 0.5
    older = k_order[None, :] < q_order[:, None]
    same = k_slots[None, :] == q_slots[:, None]
    sees = same | masked & older
    before = names[None, :] < names[:, None]
    rank = jnp.sum((sees[:, None, :] & before[None]).astype(jnp.int32), axis=-1)
    chosen = sees[:, None, :] & (rank[:, None, :] == names[None, :, None])
    listed = jnp.sum(jnp.where(chosen, names[None, None, :], 0), axis=-1)
    counts = jnp.sum(sees.astype(jnp.int32), axis=-1)
    return jnp.concatenate([listed.reshape(-1), counts, places])


def local(queries, keys, values, levels, retiring, block_mask, gates):
    span = lax.axis_index("span").astype(jnp.int32)
    token = lax.axis_index("tok").astype(jnp.int32)
    y, half, core = span // 4, span // 2 % 2, span % 2
    x, z = half * 2 + token // RING, token % RING
    hop = jnp.arange(GROUP, dtype=jnp.int32)
    target = (y + hop // 2) % 4 * 2 + (core ^ hop % 2)
    hops = [dict(dy=j // 2, core=j % 2) for j in range(GROUP)]
    backs = [dict(dy=-(j // 2), core=j % 2) for j in range(GROUP)]

    packed = call(
        pack_kernel,
        [shape(3 * ROWS + 16, WIDTH)] * GROUP,
        [SMEM, SMEM, VMEM, VMEM, VMEM],
    )(target, block_mask, queries[0], keys[0], values[0])
    shared = [packed[0]]
    for j in range(1, GROUP):
        shared.append(moved(packed[j], **hops[j]))

    shapes = []
    for part in PARTS:
        shapes += [shape(len(part) * SET, HEAD_DIM), shape(len(part) * 2 * SET, HEAD_DIM)]
    spread = call(
        spread_kernel, shapes + [shape(GROUP, HEAD_DIM, jnp.float32)], [VMEM] * GROUP
    )(*shared)

    tile = jnp.arange(TILES, dtype=jnp.int32)
    base = (y - tile // 4) % 4 * 4 + (core ^ tile // 2 % 2)
    wide_slots, near_slots = base + 2 * (tile % 2), base + 2 * half
    near_mask = jnp.repeat(spread[-1], 2, axis=0)
    other_mask = moved(spread[-1], dx=2)
    far_mask = jnp.repeat(other_mask, 2, axis=0)
    wide_mask = jnp.where((tile % 2 == half)[:, None], near_mask, far_mask)
    first = core == 0
    ring = jnp.arange(RING, dtype=jnp.int32)
    table = see_table(
        jnp.where(first, wide_slots, near_slots),
        jnp.where(first, near_slots, wide_slots),
        retiring,
        jnp.where(first, wide_mask, near_mask),
        jnp.concatenate(
            [(jnp.where(first, x, z) - ring) % RING, (jnp.where(first, z, x) - ring) % RING]
        ),
    )

    pieces = []
    for p, part in enumerate(PARTS):
        own_q, own_kv = spread[2 * p], spread[2 * p + 1]
        if p > 0:
            own_q, own_kv, table = lax.optimization_barrier((own_q, own_kv, table))
        q, kv = [own_q], [own_kv]
        for d in range(1, RING):
            kv.append(moved(own_kv, dz=d, swap=1))
        for d in range(1, RING):
            q.append(moved(own_q, dx=d, swap=1))
        parts = attend(len(part), table, q, kv)
        pieces.append(parts[0])
        for d in range(1, RING):
            pieces.append(moved(parts[d], dx=-d, swap=1))

    mixed = call(
        combine_kernel, [shape(ROWS, WIDTH)] * GROUP, [SMEM] + [VMEM] * len(pieces)
    )(table, *pieces)
    returned = [mixed[0]]
    for j in range(1, GROUP):
        returned.append(moved(mixed[j], **backs[j]))
    result = call(finish_kernel, shape(ROWS, GROUP * WIDTH), [SMEM, SMEM] + [VMEM] * (GROUP + 1))(
        target, levels, gates, *returned
    )
    return result[None]


def solution(mesh):
    return jax.shard_map(
        local,
        mesh=mesh,
        in_specs=(
            P("span", "tok", None),
            P("span", "tok", None),
            P("span", "tok", None),
            P("span"),
            P(),
            P("span", None),
            P(),
        ),
        out_specs=P("span", "tok", None),
        check_vma=False,
    )
```

```python
import functools

import jax
import jax.numpy as jnp
from jax import lax
from jax.experimental import pallas as pl
from jax.experimental.pallas import tpu as pltpu
from jax.sharding import PartitionSpec as P


HEAD_DIM = 128
SPANS = 16
ROWS = 64
GROUP = 8
HEADS_DEV = 3
WIDTH = HEADS_DEV * HEAD_DIM
RING = 4
SET = GROUP * ROWS
META = 32
PARTS = ((0, 1, 2),)
TILE = 2 * ROWS
TILES = 16
STEP = 4
SUB = 2
LOG2E = 1.4426950408889634


BOTH = ("span", "tok")
VMEM = pl.BlockSpec(memory_space=pltpu.VMEM)
SMEM = pl.BlockSpec(memory_space=pltpu.SMEM)


def device_at(x, y, z, core):
    return (y * 4 + (x // 2) * 2 + core) * 8 + (x % 2) * 4 + z


def moved(array, dx=0, dy=0, dz=0, core=0, swap=0):
    pairs = []
    for x in range(4):
        for y in range(4):
            for z in range(4):
                for c in range(2):
                    mx, mz = (dz, dx) if swap and c else (dx, dz)
                    there = device_at((x + mx) % 4, (y + dy) % 4, (z + mz) % 4, c ^ core)
                    pairs.append((device_at(x, y, z, c), there))
    return lax.ppermute(array, BOTH, pairs)


def call(kernel, shapes, specs, scratch=()):
    return pl.pallas_call(
        kernel,
        out_shape=shapes,
        in_specs=specs,
        out_specs=jax.tree.map(lambda unused: VMEM, shapes),
        scratch_shapes=scratch,
    )


def shape(rows, columns, dtype=jnp.bfloat16):
    return jax.ShapeDtypeStruct((rows, columns), dtype)


def pack_kernel(at_ref, mask_ref, q_ref, k_ref, v_ref, *out_refs):
    lanes = lax.broadcasted_iota(jnp.int32, (16, WIDTH), 1)
    meta = jnp.zeros((16, WIDTH), jnp.int32)
    for t in range(SPANS):
        meta = jnp.where(lanes == t, mask_ref[0, t], meta)
    meta = meta.astype(jnp.float32).astype(jnp.bfloat16)
    for j in range(GROUP):
        columns = pl.ds(pl.multiple_of(at_ref[j] * WIDTH, HEAD_DIM), WIDTH)
        for i, ref in enumerate((q_ref, k_ref, v_ref)):
            out_refs[j][i * ROWS : (i + 1) * ROWS, :] = ref[:, columns]
        out_refs[j][3 * ROWS :, :] = meta


def spread_kernel(*refs):
    in_refs, out_refs = refs[:GROUP], refs[GROUP:]
    for j in range(GROUP):
        ref = in_refs[j]
        for p, part in enumerate(PARTS):
            q_ref, kv_ref = out_refs[2 * p], out_refs[2 * p + 1]
            for i, h in enumerate(part):
                columns = slice(h * HEAD_DIM, (h + 1) * HEAD_DIM)
                q_ref[i * SET + j * ROWS : i * SET + (j + 1) * ROWS, :] = ref[0:ROWS, columns]
                for t in range(2):
                    base = (2 * i + t) * SET + j * ROWS
                    kv_ref[base : base + ROWS, :] = ref[(t + 1) * ROWS : (t + 2) * ROWS, columns]
        row = ref[3 * ROWS : 3 * ROWS + 16, 0:HEAD_DIM].astype(jnp.float32)
        out_refs[-1][j : j + 1, :] = row[0:1]


def together_in(count):
    return 2 if count == 1 else 1


def attend_kernel(count, table_ref, *refs):
    together = together_in(count)
    q_refs, kv_refs = refs[:RING], refs[RING : 2 * RING]
    out_refs = refs[2 * RING : 3 * RING]
    q_all, k_all, v_all, o_all, v_turned, score_ref, lse_ref = refs[3 * RING :]
    factor = jnp.float32(HEAD_DIM ** (-0.5) * LOG2E)

    def rows_of(ref, h, i):
        return ref[h, i // 2, pl.ds(i % 2 * 2, 2)].reshape(TILE, HEAD_DIM)

    limits = TILES * TILES
    q_place = [table_ref[limits + TILES + d] for d in range(RING)]
    k_place = [table_ref[limits + TILES + RING + d] for d in range(RING)]
    for h in range(count):
        for d in range(RING):
            q_all[h, :, q_place[d]] = q_refs[d][h]
            k_all[h, :, k_place[d]] = kv_refs[d][h, 0]
            v_all[h, :, k_place[d]] = kv_refs[d][h, 1]
    for h in range(count):
        for i in range(TILES):
            rows = slice(i * TILE, (i + 1) * TILE)
            v_turned[h, :, rows] = rows_of(v_all, h, i).T

    chains = [(t, h) for t in range(together) for h in range(count)]

    def trips_of(first):
        seen = [table_ref[limits + first * together + t] for t in range(together)]
        return jnp.maximum((functools.reduce(jnp.maximum, seen) + STEP - 1) // STEP, 1)

    def fill(first, g):
        for c, (t, h) in enumerate(chains):
            pick = first * together + t
            at = pick * TILES + g * STEP
            rows = [rows_of(k_all, h, table_ref[at + u]) for u in range(STEP)]
            score_ref[c] = lax.dot_general(
                jnp.concatenate(rows, axis=0),
                rows_of(q_all, h, pick),
                (((1,), (1,)), ((), ())),
                preferred_element_type=jnp.float32,
            )

    def tiles(first, unused):
        picks = [first * together + t for t in range(together)]
        seen = [table_ref[limits + i] for i in picks]
        trips = trips_of(first)
        starts = [pl.multiple_of(i * TILE, TILE) for i in picks]

        def place(t, g, u):
            return table_ref[picks[t] * TILES + g * STEP + u]

        def step(g, carry):
            parts = [range(at, at + SUB) for at in range(0, STEP, SUB)]
            scores = [score_ref[c] for c in range(len(chains))]
            last = (g + 1 >= trips).astype(jnp.int32)
            fill(jnp.minimum(first + last, TILES // together - 1), (1 - last) * (g + 1))
            result = list(carry)
            for part in parts:
                for c, (t, h) in enumerate(chains):
                    top, total, acc = result[c]
                    score = scores[c][part[0] * TILE : (part[-1] + 1) * TILE]
                    blocks = []
                    for n, u in enumerate(part):
                        block = score[n * TILE : (n + 1) * TILE]
                        blocks.append(jnp.where(g * STEP + u < seen[t], block, -1e30))
                    largest = functools.reduce(jnp.maximum, blocks)
                    new_top = jnp.maximum(top, jnp.max(largest, axis=0, keepdims=True))
                    shrink = jnp.exp2((top - new_top) * factor)
                    weights = [jnp.exp2((block - new_top) * factor) for block in blocks]
                    added = functools.reduce(jnp.add, weights).reshape(TILE // 8, 8, TILE)
                    total = total * shrink + jnp.sum(added, axis=0)
                    weight = jnp.concatenate([w.astype(jnp.bfloat16) for w in weights], axis=0)
                    ats = [pl.multiple_of(place(t, g, u) * TILE, TILE) for u in part]
                    columns = [v_turned[h, :, pl.ds(at, TILE)] for at in ats]
                    acc = acc * shrink + jnp.dot(
                        jnp.concatenate(columns, axis=1),
                        weight,
                        preferred_element_type=jnp.float32,
                    )
                    result[c] = (new_top, total, acc)
            return result

        empty = (
            jnp.full((1, TILE), -1e30, jnp.float32),
            jnp.zeros((8, TILE), jnp.float32),
            jnp.zeros((HEAD_DIM, TILE), jnp.float32),
        )
        final = lax.fori_loop(0, trips, step, [empty] * len(chains))
        for (t, h), (top, total, acc) in zip(chains, final):
            total = jnp.sum(total, axis=0, keepdims=True)
            total = jnp.where(total > 0.0, total, 1.0)
            o_all[h, pl.ds(starts[t], TILE), :] = (acc * (1.0 / total)).T.astype(jnp.bfloat16)
            lse_ref[h, picks[t] % 2, pl.ds(picks[t] // 2, 1), :] = top * factor + jnp.log2(total)
        return unused

    fill(0, 0)
    lax.fori_loop(0, TILES // together, tiles, 0)
    for h in range(count):
        for d in range(RING):
            base = h * (SET + META)
            for j in range(GROUP):
                at = pl.multiple_of(j * RING * ROWS + q_place[d] * ROWS, ROWS)
                out_refs[d][base + j * ROWS : base + (j + 1) * ROWS, :] = o_all[
                    h, pl.ds(at, ROWS), :
                ]
            value = lse_ref[h, q_place[d] // 2]
            high = value.astype(jnp.bfloat16).astype(jnp.float32)
            middle = (value - high).astype(jnp.bfloat16).astype(jnp.float32)
            low = value - high - middle
            out_refs[d][base + SET : base + SET + META, :] = jnp.concatenate(
                [high, middle, low, jnp.zeros_like(low)], axis=0
            ).astype(jnp.bfloat16)


def attend(count, table, q, kv):
    q = [piece.reshape(count, GROUP, ROWS, HEAD_DIM) for piece in q]
    kv = [piece.reshape(count, 2, GROUP, ROWS, HEAD_DIM) for piece in kv]
    pieces = pltpu.VMEM((count, GROUP, RING, ROWS, HEAD_DIM), jnp.bfloat16)
    return call(
        functools.partial(attend_kernel, count),
        [shape(count * (SET + META), HEAD_DIM)] * RING,
        [SMEM] + [VMEM] * (2 * RING),
        [pieces] * 3
        + [
            pltpu.VMEM((count, RING * SET, HEAD_DIM), jnp.bfloat16),
            pltpu.VMEM((count, HEAD_DIM, RING * SET), jnp.bfloat16),
            pltpu.VMEM((count * together_in(count), STEP * TILE, TILE), jnp.float32),
            pltpu.VMEM((count, 2, GROUP, HEAD_DIM), jnp.float32),
        ],
    )(table, *q, *kv)


def combine_kernel(table_ref, *refs):
    out_refs = refs[-GROUP:]
    shift = table_ref[TILES * TILES + TILES] % 2 * ROWS
    lanes = lax.broadcasted_iota(jnp.int32, (ROWS, HEAD_DIM), 1)
    eye = lanes == lax.broadcasted_iota(jnp.int32, (ROWS, HEAD_DIM), 0) + shift
    for p, part in enumerate(PARTS):
        pieces = refs[p * RING : (p + 1) * RING]
        for i, h in enumerate(part):
            base = i * (SET + META)
            lse = []
            for ref in pieces:
                coded = ref[base + SET : base + SET + META, :].astype(jnp.float32)
                lse.append(coded[0:8] + coded[8:16] + coded[16:24])
            top = functools.reduce(jnp.maximum, lse)
            shares = [jnp.exp2(value - top) for value in lse]
            total = functools.reduce(jnp.add, shares)
            shares = [value / total for value in shares]
            for j in range(GROUP):
                mixed = jnp.zeros((ROWS, HEAD_DIM), jnp.float32)
                for ref, share in zip(pieces, shares):
                    column = jnp.sum(jnp.where(eye, share[j : j + 1], 0.0), axis=1, keepdims=True)
                    rows = ref[base + j * ROWS : base + (j + 1) * ROWS, :]
                    mixed = mixed + column * rows.astype(jnp.float32)
                out_refs[j][:, h * HEAD_DIM : (h + 1) * HEAD_DIM] = mixed.astype(jnp.bfloat16)


def finish_kernel(at_ref, level_ref, gates_ref, *refs):
    out_ref = refs[-1]
    for j in range(GROUP):
        columns = pl.ds(pl.multiple_of(at_ref[j] * WIDTH, HEAD_DIM), WIDTH)
        gate = gates_ref[pl.ds(level_ref[0], 1), columns]
        out_ref[:, columns] = (refs[j][...].astype(jnp.float32) * gate).astype(jnp.bfloat16)


def see_table(q_slots, k_slots, retiring, mask, places):
    names = jnp.arange(TILES, dtype=jnp.int32)
    q_order = (q_slots - retiring[0]) % SPANS
    k_order = (k_slots - retiring[0]) % SPANS
    slots = jnp.arange(SPANS, dtype=jnp.int32)
    picked = (k_slots[:, None] == slots[None, :]).astype(jnp.float32)
    masked = jnp.sum(mask[:, None, :SPANS] * picked[None], axis=-1) > 0.5
    older = k_order[None, :] < q_order[:, None]
    same = k_slots[None, :] == q_slots[:, None]
    sees = same | masked & older
    before = names[None, :] < names[:, None]
    rank = jnp.sum((sees[:, None, :] & before[None]).astype(jnp.int32), axis=-1)
    chosen = sees[:, None, :] & (rank[:, None, :] == names[None, :, None])
    listed = jnp.sum(jnp.where(chosen, names[None, None, :], 0), axis=-1)
    counts = jnp.sum(sees.astype(jnp.int32), axis=-1)
    return jnp.concatenate([listed.reshape(-1), counts, places])


def local(queries, keys, values, levels, retiring, block_mask, gates):
    span = lax.axis_index("span").astype(jnp.int32)
    token = lax.axis_index("tok").astype(jnp.int32)
    y, half, core = span // 4, span // 2 % 2, span % 2
    x, z = half * 2 + token // RING, token % RING
    hop = jnp.arange(GROUP, dtype=jnp.int32)
    target = (y + hop // 2) % 4 * 2 + (core ^ hop % 2)
    hops = [dict(dy=j // 2, core=j % 2) for j in range(GROUP)]
    backs = [dict(dy=-(j // 2), core=j % 2) for j in range(GROUP)]

    packed = call(
        pack_kernel,
        [shape(3 * ROWS + 16, WIDTH)] * GROUP,
        [SMEM, SMEM, VMEM, VMEM, VMEM],
    )(target, block_mask, queries[0], keys[0], values[0])
    shared = [packed[0]]
    for j in range(1, GROUP):
        shared.append(moved(packed[j], **hops[j]))

    shapes = []
    for part in PARTS:
        shapes += [shape(len(part) * SET, HEAD_DIM), shape(len(part) * 2 * SET, HEAD_DIM)]
    spread = call(
        spread_kernel, shapes + [shape(GROUP, HEAD_DIM, jnp.float32)], [VMEM] * GROUP
    )(*shared)

    tile = jnp.arange(TILES, dtype=jnp.int32)
    base = (y - tile // 4) % 4 * 4 + (core ^ tile // 2 % 2)
    wide_slots, near_slots = base + 2 * (tile % 2), base + 2 * half
    near_mask = jnp.repeat(spread[-1], 2, axis=0)
    far_mask = jnp.repeat(moved(spread[-1], dx=2), 2, axis=0)
    wide_mask = jnp.where((tile % 2 == half)[:, None], near_mask, far_mask)
    first = core == 0
    ring = jnp.arange(RING, dtype=jnp.int32)
    table = see_table(
        jnp.where(first, wide_slots, near_slots),
        jnp.where(first, near_slots, wide_slots),
        retiring,
        jnp.where(first, wide_mask, near_mask),
        jnp.concatenate(
            [(jnp.where(first, x, z) - ring) % RING, (jnp.where(first, z, x) - ring) % RING]
        ),
    )

    pieces = []
    for p, part in enumerate(PARTS):
        own_q, own_kv = spread[2 * p], spread[2 * p + 1]
        if p > 0:
            own_q, own_kv, table = lax.optimization_barrier((own_q, own_kv, table))
        q, kv = [own_q], [own_kv]
        for d in range(1, RING):
            kv.append(moved(own_kv, dz=d, swap=1))
        for d in range(1, RING):
            q.append(moved(own_q, dx=d, swap=1))
        parts = attend(len(part), table, q, kv)
        pieces.append(parts[0])
        for d in range(1, RING):
            pieces.append(moved(parts[d], dx=-d, swap=1))

    mixed = call(
        combine_kernel, [shape(ROWS, WIDTH)] * GROUP, [SMEM] + [VMEM] * len(pieces)
    )(table, *pieces)
    returned = [mixed[0]]
    for j in range(1, GROUP):
        returned.append(moved(mixed[j], **backs[j]))
    result = call(finish_kernel, shape(ROWS, GROUP * WIDTH), [SMEM, SMEM] + [VMEM] * (GROUP + 1))(
        target, levels, gates, *returned
    )
    return result[None]


def solution(mesh):
    return jax.shard_map(
        local,
        mesh=mesh,
        in_specs=(
            P("span", "tok", None),
            P("span", "tok", None),
            P("span", "tok", None),
            P("span"),
            P(),
            P("span", None),
            P(),
        ),
        out_specs=P("span", "tok", None),
        check_vma=False,
    )
```
